32 devices in a mesh: parts: 2 (over y), tm: 4 (over z), head: 2 (over x), sub: 2 (over core).
Axes of the slice: x: 2, y: 2, z: 4, core: 2. Of those that a mesh axis runs over, the one named last changes fastest.
Arguments:
- signal: bfloat16 [32768, 2048], P(('parts', 'tm'), ('head', 'sub')), parts along dimension 0, may hold values from -6 to 6
- entry_map: bfloat16 [32768, 128], P(('parts', 'tm')), parts along dimension 0, may hold values from -6 to 6
- readout: bfloat16 [32768, 128], P(('parts', 'tm')), parts along dimension 0, may hold values from -6 to 6
- gate_input: bfloat16 [32768, 2048], P(('parts', 'tm'), ('head', 'sub')), parts along dimension 0, may hold values from -40 to 40
- log_decay: float32 [32, 32768], P(('head', 'sub'), ('parts', 'tm')), parts along dimension 1, may hold values from -0.6 to 0, as said below
- norm_gain: float32 [2048], P(('head', 'sub')), may hold values from 0.5 to 1.5
Outputs:
- layer_out: bfloat16 [32768, 2048], P(('parts', 'tm'), ('head', 'sub')), parts along dimension 0
The draws below stay inside these ranges and needn't reach their ends.
There are 2 independent parts, one for each index of `parts`. The reference program is written for one: setup_inputs(seed, part) draws one part's arguments, and reference() takes and returns one part's arrays. A program takes and returns all parts, laid end to end along the dimension named above; an argument that names none is the same for every part. Nothing has to cross between parts.
Inputs may be any that keep to these rules, and one draw needn't show every extreme that they name: `log_decay`: never positive.
All inputs are finite; a program needn't handle non-finite values.
Results may differ from the reference program's by a relative error of at most 0.0075.
Values sent between devices are 32-bit elements; how exact they have to be, the bound alone decides.
No kernel may reach another device: no remote copies, remote signals or barrier semaphores. Data moves between devices by JAX's collectives and lax.ppermute only.
A program may use at most 128 MiB of HBM per device.

```python
import math
import jax
import jax.numpy as jnp
from jax import lax

H = 32
P_SIZE = 64
N = 128
SPAN = 256
FRAMES = 16384


def draw_log_decay(key, part):
    keys = jax.random.split(jax.random.fold_in(key, 11), 6)
    share = 0.5
    is_fast = jax.random.bernoulli(keys[0], share, (H, 1))
    fast_rates = jnp.exp(jax.random.uniform(keys[1], (H, 1), minval=math.log(1.0 / 50.0), maxval=math.log(1.0 / 30.0)))
    slow_rates = jnp.exp(jax.random.uniform(keys[2], (H, 1), minval=math.log(0.05), maxval=math.log(0.2))) / FRAMES
    fading_speeds = jnp.where(is_fast, fast_rates, slow_rates)
    stochastic_shift = jnp.exp(jax.random.uniform(keys[3], (H, FRAMES), minval=-math.log(2.0), maxval=math.log(2.0)))
    third = FRAMES // 3
    offsets = jax.random.randint(keys[4], (H, 3, 1), 0, third)
    waveform_locations = offsets + (jnp.arange(3) * third)[None, :, None]
    lost_audio_slices = jax.random.uniform(keys[5], (H, 3, 1), minval=0.22, maxval=0.51)
    slice_location_number = jnp.arange(FRAMES)[None, None, :]
    spike_occurrences = jnp.sum(jnp.where(slice_location_number == waveform_locations, lost_audio_slices, 0.0), axis=1)
    return (-(fading_speeds * stochastic_shift) - spike_occurrences).astype(jnp.float32)


def draw_gate_input(key, part):
    keys = jax.random.split(jax.random.fold_in(key, 7), 3)
    rows = jnp.exp(jax.random.uniform(keys[0], (FRAMES, 1), minval=-1.15, maxval=1.15))
    columns = jnp.exp(jax.random.uniform(keys[1], (1, H * P_SIZE), minval=-1.15, maxval=1.15))
    smooth = jax.random.truncated_normal(keys[2], -4.0, 4.0, (FRAMES, H * P_SIZE))
    return (smooth * rows * columns).astype(jnp.bfloat16)


def block_levels(stream_key, dims, pieces, smallest, largest):
    def one(axis_at, shards_of):
        heights = jax.random.uniform(jax.random.fold_in(jax.random.fold_in(stream_key, 6), axis_at), (shards_of,), jnp.float32, smallest / len(pieces), largest / len(pieces))
        return jnp.repeat(jnp.exp(heights), dims[axis_at] // shards_of).reshape((-1,) + (1,) * (len(dims) - axis_at - 1))

    gain = one(*pieces[0])
    for cut in pieces[1:]:
        gain = gain * one(*cut)
    return gain


def noise(own_key, shape, scale, most, cuts=(), held_as=jnp.bfloat16):
    values = scale * jax.random.normal(own_key, shape, jnp.float32)
    if cuts:
        values = values * block_levels(own_key, shape, cuts, -0.22, 0.18)
    return jnp.clip(values, -most, most).astype(held_as)


def setup_inputs(seed: int = 0, part: int = 0) -> dict:
    streams_of = jax.random.split(jax.random.key(seed), 7)
    part_splits = jax.random.split(jax.random.fold_in(streams_of[6], part), 7)
    return {
        "signal": noise(part_splits[0], (FRAMES, H * P_SIZE), 1.0, 6.0, ((0, 4), (1, 4))),
        "entry_map": noise(part_splits[1], (FRAMES, N), 1.0, 6.0, ((0, 4),)),
        "readout": noise(part_splits[2], (FRAMES, N), 1.0, 6.0, ((0, 4),)),
        "gate_input": draw_gate_input(jax.random.fold_in(jax.random.fold_in(streams_of[6], part), 71), part),
        "log_decay": draw_log_decay(jax.random.fold_in(jax.random.fold_in(streams_of[6], part), 71), part),
        "norm_gain": jnp.clip(1.0 + 0.1 * jax.random.normal(streams_of[5], (H * P_SIZE,), jnp.float32), 0.5, 1.5),
    }


epsilon = 1e-05

def single_head(scores, entries, readouts, causal, signal, gate_input, log_decay, norm_gain):
    blocks = scores.shape[0]
    signals = signal.reshape(blocks, SPAN, P_SIZE)
    running = jnp.cumsum(log_decay.reshape(blocks, SPAN), axis=1)
    spread = running[:, :, None] - running[:, None, :]
    decays = jnp.where(causal, jnp.exp(jnp.where(causal, spread, 0.0)), 0.0)
    weights = (scores * decays).astype(jnp.bfloat16)
    inside = jnp.einsum('cts,csp->ctp', weights.astype(jnp.float32), signals.astype(jnp.float32))
    remains = jnp.exp(running[:, -1:] - running)
    written = (entries.astype(jnp.float32) * remains[:, :, None]).astype(jnp.bfloat16)
    states = jnp.einsum('csp,csn->cpn', signals.astype(jnp.float32), written.astype(jnp.float32))
    totals = running[:, -1]

    def advance(carried, element):
        block_total, block_state = element
        return (jnp.exp(block_total) * carried + block_state, carried)
    _, incoming = lax.scan(advance, jnp.zeros((P_SIZE, N), jnp.float32), (totals, states))
    across = jnp.einsum('ctn,cpn->ctp', readouts.astype(jnp.float32), incoming, precision=lax.Precision.HIGHEST)
    across = across * jnp.exp(running)[:, :, None]
    output = (inside + across).reshape(blocks * SPAN, P_SIZE)
    gated_out = output * jax.nn.silu(gate_input.astype(jnp.float32))
    scaled = gated_out * lax.rsqrt(lax.optimization_barrier(jnp.mean(gated_out * gated_out, axis=-1, keepdims=True)) + epsilon)
    return (scaled * norm_gain).astype(jnp.bfloat16)

def reference(signal, entry_map, readout, gate_input, log_decay, norm_gain):
    blocks = FRAMES // SPAN
    entries = entry_map.reshape(blocks, SPAN, N)
    readouts = readout.reshape(blocks, SPAN, N)
    scores = jnp.einsum('ctn,csn->cts', readouts.astype(jnp.float32), entries.astype(jnp.float32))
    causal = jnp.tril(jnp.ones((SPAN, SPAN), bool))
    per_head = (signal.reshape(FRAMES, H, P_SIZE).transpose(1, 0, 2), gate_input.reshape(FRAMES, H, P_SIZE).transpose(1, 0, 2), log_decay, norm_gain.reshape(H, P_SIZE))
    result = lax.map(lambda element: single_head(scores, entries, readouts, causal, element[0], element[1], element[2], element[3]), per_head)
    return result.transpose(1, 0, 2).reshape(FRAMES, H * P_SIZE)
```

```python
import functools

import jax
import jax.numpy as jnp
from jax import lax
from jax.experimental import pallas as pl
from jax.experimental.pallas import tpu as pltpu
from jax.sharding import PartitionSpec as P

CHUNK = 128
HEAD_ROWS = 8
EPSILON = 1e-05
F32 = jnp.float32
BF16 = jnp.bfloat16
TN = (((0,), (0,)), ((), ()))
NT = (((1,), (1,)), ((), ()))


def mm(left, right, dims=(((1,), (0,)), ((), ()))):
    return lax.dot_general(left, right, dims, preferred_element_type=F32)


def two_terms(value):
    high = value.astype(BF16)
    return high, (value - high.astype(F32)).astype(BF16)


def spread_matrix(width, head_size):
    row = lax.broadcasted_iota(jnp.int32, (2 * HEAD_ROWS, width), 0)
    column = lax.broadcasted_iota(jnp.int32, (2 * HEAD_ROWS, width), 1)
    own = lax.rem(row, HEAD_ROWS) == lax.div(column, head_size)
    return own.astype(F32).astype(BF16)


def stacked(decay):
    chunks = decay.shape[1] // CHUNK
    return jnp.concatenate([decay[:, c * CHUNK : (c + 1) * CHUNK] for c in range(chunks)], axis=0)


def sums(decay_rows, matrix):
    high = decay_rows.astype(BF16)
    rest = decay_rows - high.astype(F32)
    middle = rest.astype(BF16)
    low = (rest - middle.astype(F32)).astype(BF16)
    return mm(high, matrix) + (mm(middle, matrix) + mm(low, matrix))


def pair_rows(value):
    high, low = two_terms(value)
    return jnp.concatenate([high, low], axis=0)


def indicator(test):
    return test.astype(F32).astype(BF16)


def state_kernel(split, head_size, place_ref, decay_ref, entry_ref, signal_ref, *rest):
    outs, (factor_ref, total_ref, state_ref) = rest[:-3], rest[-3:]
    step = pl.program_id(0)
    rows, width = signal_ref.shape
    per_tile = rows // CHUNK
    spread = spread_matrix(width, head_size)

    @pl.when(step == 0)
    def _():
        tall = stacked(decay_ref[...])
        chunks = tall.shape[0] // HEAD_ROWS
        s_from = lax.broadcasted_iota(jnp.int32, (CHUNK, 2 * CHUNK), 0)
        s_to = lax.broadcasted_iota(jnp.int32, (CHUNK, 2 * CHUNK), 1)
        both = sums(tall, indicator((s_from > s_to) | (s_to >= CHUNK)))
        later = jnp.zeros((HEAD_ROWS, CHUNK), F32)
        for c in reversed(range(chunks)):
            part = both[c * HEAD_ROWS : (c + 1) * HEAD_ROWS]
            factor_ref[c] = pair_rows(jnp.exp(part[:, :CHUNK] + later))
            later = later + part[:, CHUNK:]
        total_ref[...] = later
        state_ref[...] = jnp.zeros_like(state_ref)

    added = None
    for start in range(0, per_tile, 2):
        many = min(2, per_tile - start)
        where = pl.ds(start * CHUNK, many * CHUNK)
        factor = jnp.concatenate(
            [mm(factor_ref[step * per_tile + start + k], spread, TN) for k in range(many)], axis=0
        )
        scaled = (signal_ref[where, :].astype(F32) * factor).astype(BF16)
        term = mm(entry_ref[where, :], scaled, TN)
        added = term if added is None else added + term
    state_ref[...] += added

    @pl.when(step == pl.num_programs(0) - 1)
    def _():
        gain = mm(pair_rows(jnp.exp(total_ref[:, :HEAD_ROWS])), spread, TN)
        states = state_ref[...]
        size = states.shape[0]
        if split:
            own_ref, first_ref, second_ref = outs
            half = width // 2
            place = place_ref[0]
            for k in range(2):
                own_ref[k, :size, :] = states[:, k * half : (k + 1) * half]
                own_ref[k, size:, :] = gain[:, k * half : (k + 1) * half]

            @pl.when(place == 0)
            def _():
                first_ref[...] = own_ref[0]
                second_ref[...] = own_ref[1]

            @pl.when(place != 0)
            def _():
                first_ref[...] = own_ref[1]
                second_ref[...] = own_ref[0]
        else:
            (own_ref,) = outs
            own_ref[:size, :] = states
            own_ref[size:, :] = gain


def local_states(place, decay, entry_map, signal, head_size, split, tile):
    length, width = signal.shape
    state_size = entry_map.shape[1]
    tall = state_size + HEAD_ROWS
    if split:
        shapes = [(2, tall, width // 2), (tall, width // 2), (tall, width // 2)]
    else:
        shapes = [(tall, width)]
    whole = [pl.BlockSpec(s, functools.partial(lambda r, i: (0,) * r, len(s))) for s in shapes]
    return pl.pallas_call(
        functools.partial(state_kernel, split, head_size),
        grid=(length // tile,),
        in_specs=[
            pl.BlockSpec(memory_space=pltpu.SMEM),
            pl.BlockSpec((HEAD_ROWS, length), lambda i: (0, 0)),
            pl.BlockSpec((tile, state_size), lambda i: (i, 0)),
            pl.BlockSpec((tile, width), lambda i: (i, 0)),
        ],
        out_specs=whole,
        out_shape=[jax.ShapeDtypeStruct(s, F32) for s in shapes],
        scratch_shapes=[
            pltpu.VMEM((length // CHUNK, 2 * HEAD_ROWS, CHUNK), BF16),
            pltpu.VMEM((HEAD_ROWS, CHUNK), F32),
            pltpu.VMEM((state_size, width), F32),
        ],
        name="device_states",
        cost_estimate=pl.CostEstimate(
            flops=2 * length * width * state_size,
            bytes_accessed=2 * length * (width + state_size),
            transcendentals=0,
        ),
    )(place, decay, entry_map, signal)


def local_kernel(base, head_size, decay_ref, entry_ref, readout_ref, signal_ref, gate_ref, state_in, *rest):
    inside_ref, share_ref, state_ref, in_ref, out_ref, whole_ref, step_ref = rest[-7:]
    step = pl.program_id(0)
    rows, width = signal_ref.shape
    per_tile = rows // CHUNK
    spread = spread_matrix(width, head_size)

    @pl.when(step == 0)
    def _():
        tall = stacked(decay_ref[...])
        chunks = tall.shape[0] // HEAD_ROWS
        half = CHUNK // 2
        s_from = lax.broadcasted_iota(jnp.int32, (CHUNK, CHUNK), 0)
        s_to = lax.broadcasted_iota(jnp.int32, (CHUNK, CHUNK), 1)
        first = (s_from < half).astype(F32)
        centred = ((s_from <= s_to).astype(F32) - first).astype(BF16)
        matrix = jnp.concatenate([centred, first.astype(BF16), (1.0 - first).astype(BF16)], axis=1)
        three = sums(tall, matrix)
        before = jnp.zeros((HEAD_ROWS, CHUNK), F32)
        for c in range(chunks):
            part = three[c * HEAD_ROWS : (c + 1) * HEAD_ROWS]
            from_middle = part[:, :CHUNK]
            to_middle = part[:, CHUNK : 2 * CHUNK]
            onward = part[:, 2 * CHUNK :]
            in_ref[c] = pair_rows(jnp.exp(-from_middle))
            out_ref[c] = pair_rows(jnp.exp(from_middle))
            whole_ref[c] = pair_rows(jnp.exp(before + (to_middle + from_middle)))
            if c + 1 < chunks:
                following = three[(c + 1) * HEAD_ROWS : (c + 2) * HEAD_ROWS, CHUNK : 2 * CHUNK]
                step_ref[c] = pair_rows(jnp.exp(onward + following))
            else:
                step_ref[c] = pair_rows(jnp.exp(onward))
            before = before + (to_middle + onward)
        state_ref[...] = state_in[...]

    t_row = lax.broadcasted_iota(jnp.int32, (CHUNK, CHUNK), 0)
    s_column = lax.broadcasted_iota(jnp.int32, (CHUNK, CHUNK), 1)
    causal = t_row >= s_column
    state = state_ref[...]
    for k in range(per_tile):
        c = base + step * per_tile + k
        where = pl.ds(k * CHUNK, CHUNK)
        entry = entry_ref[where, :]
        readout = readout_ref[where, :]
        scaled = (signal_ref[where, :].astype(F32) * mm(in_ref[c], spread, TN)).astype(BF16)
        scores = jnp.where(causal, mm(readout, entry, NT), 0.0).astype(BF16)
        left = jnp.concatenate([scores, readout], axis=1)
        right = jnp.concatenate([scaled, state.astype(BF16)], axis=0)
        output = mm(left, right) * mm(out_ref[c], spread, TN)
        state = state + mm(entry, scaled, TN)
        onward = mm(step_ref[c][:, :HEAD_ROWS], spread, TN)
        size = state.shape[0]
        state = (state.reshape(size // HEAD_ROWS, HEAD_ROWS, width) * onward[None]).reshape(size, width)
        gate = gate_ref[where, :].astype(F32)
        silu = gate / (1.0 + jnp.exp(-gate))
        inside_ref[where, :] = (output * silu).astype(BF16)
        share_ref[where, :] = (silu * mm(whole_ref[c], spread, TN)).astype(BF16)
    state_ref[...] = state


def local_part(index, parts, decay, entry_map, readout, signal, gate_input, state, kept, head_size, tile):
    length, width = signal.shape
    state_size = entry_map.shape[1]
    tiles = length // tile // parts
    first = index * tiles
    row_block = lambda i: (i + first, 0)
    fixed = lambda i: (0, 0)
    in_specs = [
        pl.BlockSpec((HEAD_ROWS, length), fixed),
        pl.BlockSpec((tile, state_size), row_block),
        pl.BlockSpec((tile, state_size), row_block),
        pl.BlockSpec((tile, width), row_block),
        pl.BlockSpec((tile, width), row_block),
        pl.BlockSpec((state_size, width), fixed),
    ]
    arguments = [decay, entry_map, readout, signal, gate_input, state]
    aliases = {}
    if kept is not None:
        aliases = {len(arguments): 0, len(arguments) + 1: 1}
        arguments += list(kept)
        in_specs += [pl.BlockSpec(memory_space=pl.ANY)] * 2
    chunks = length // CHUNK
    return pl.pallas_call(
        functools.partial(local_kernel, first * (tile // CHUNK), head_size),
        grid=(tiles,),
        in_specs=in_specs,
        out_specs=[
            pl.BlockSpec((tile, width), row_block),
            pl.BlockSpec((tile, width), row_block),
            pl.BlockSpec((state_size, width), fixed),
        ],
        out_shape=[
            jax.ShapeDtypeStruct((length, width), BF16),
            jax.ShapeDtypeStruct((length, width), BF16),
            jax.ShapeDtypeStruct((state_size, width), F32),
        ],
        input_output_aliases=aliases,
        scratch_shapes=[pltpu.VMEM((chunks, 2 * HEAD_ROWS, CHUNK), BF16)] * 4,
        name="local_part",
        cost_estimate=pl.CostEstimate(
            flops=8 * length * width * state_size // parts,
            bytes_accessed=2 * length * (4 * width + 2 * state_size) // parts,
            transcendentals=length * width // parts,
        ),
    )(*arguments)


def final_kernel(split, head_size, place_ref, *rest):
    count = 3 if split else 1
    incoming = rest[:count]
    readout_ref, inside_ref, share_ref, gain_ref, result_ref, terms_ref = rest[count:]
    size = readout_ref.shape[1]
    width = inside_ref.shape[1]

    def keep(value, at):
        high, low = two_terms(value)
        terms_ref[:size, at : at + value.shape[1]] = high
        terms_ref[size:, at : at + value.shape[1]] = low

    @pl.when(pl.program_id(0) == 0)
    def _():
        if split:
            one, two, kept = incoming
            place = place_ref[0]
            half = width // 2

            @pl.when(place == 1)
            def _():
                keep(kept[...], 0)
                keep(two[...], half)

            @pl.when(place == 2)
            def _():
                keep(one[...], 0)
                keep(kept[...], half)

            @pl.when((place != 1) & (place != 2))
            def _():
                keep(two[...], 0)
                keep(one[...], half)
        else:
            keep(incoming[0][...], 0)

    group = min(width, 256)
    row = lax.broadcasted_iota(jnp.int32, (group, group), 0)
    column = lax.broadcasted_iota(jnp.int32, (group, group), 1)
    same = lax.div(row, head_size) == lax.div(column, head_size)
    average = jnp.where(same, 1.0 / head_size, 0.0).astype(BF16)
    readout = readout_ref[...]
    across = mm(jnp.concatenate([readout, readout], axis=1), terms_ref[...])
    gated = inside_ref[...].astype(F32) + share_ref[...].astype(F32) * across
    squares = (gated * gated).astype(BF16)
    mean = jnp.concatenate(
        [mm(squares[:, g : g + group], average) for g in range(0, width, group)], axis=1
    )
    result_ref[...] = (gated * lax.rsqrt(mean + EPSILON) * gain_ref[...]).astype(BF16)


def final_part(place, incoming, readout, inside, share, norm_gain, head_size, split, tile):
    length, width = inside.shape
    state_size = readout.shape[1]
    row_block = lambda i: (i, 0)
    fixed = lambda i: (0, 0)
    return pl.pallas_call(
        functools.partial(final_kernel, split, head_size),
        grid=(length // tile,),
        in_specs=[pl.BlockSpec(memory_space=pltpu.SMEM)]
        + [pl.BlockSpec(v.shape, fixed) for v in incoming]
        + [
            pl.BlockSpec((tile, state_size), row_block),
            pl.BlockSpec((tile, width), row_block),
            pl.BlockSpec((tile, width), row_block),
            pl.BlockSpec((1, width), fixed),
        ],
        out_specs=pl.BlockSpec((tile, width), row_block),
        out_shape=jax.ShapeDtypeStruct((length, width), BF16),
        scratch_shapes=[pltpu.VMEM((2 * state_size, width), BF16)],
        name="final_part",
        cost_estimate=pl.CostEstimate(
            flops=4 * length * width * state_size,
            bytes_accessed=2 * length * (3 * width + state_size),
            transcendentals=length * width,
        ),
    )(place, *incoming, readout, inside, share, norm_gain)


def blend_kernel(place_ref, one_ref, two_ref, own_ref, first_ref, second_ref, kept_ref):
    size = kept_ref.shape[0]
    width = kept_ref.shape[1]

    def scaled(rows_ref, value):
        gain = rows_ref[size:, :]
        shape = (size // HEAD_ROWS, HEAD_ROWS, width)
        return (value.reshape(shape) * gain[None]).reshape(size, width)

    @pl.when(place_ref[0] == 1)
    def _():
        mine = own_ref.at[0]
        first = one_ref[:size, :]
        second = mine[:size, :] + scaled(mine, first)
        first_ref[...] = second
        second_ref[...] = two_ref[:size, :] + scaled(two_ref, second)
        kept_ref[...] = first

    @pl.when(place_ref[0] != 1)
    def _():
        mine = own_ref.at[1]
        first = two_ref[:size, :]
        second = one_ref[:size, :] + scaled(one_ref, first)
        first_ref[...] = mine[:size, :] + scaled(mine, second)
        second_ref[...] = first
        kept_ref[...] = second


def blend(place, one, two, own):
    size = one.shape[0] - HEAD_ROWS
    width = one.shape[1]
    return pl.pallas_call(
        blend_kernel,
        in_specs=[pl.BlockSpec(memory_space=pltpu.SMEM)] + [pl.BlockSpec(memory_space=pltpu.VMEM)] * 3,
        out_specs=[pl.BlockSpec(memory_space=pltpu.VMEM)] * 3,
        out_shape=[jax.ShapeDtypeStruct((size, width), F32)] * 3,
        name="blend",
    )(place, one, two, own)


def scan_devices(own, devices):
    size = own.shape[0] - HEAD_ROWS
    gain = lambda v: v[size : size + 1]
    reach, before = own, None
    shift = 1
    while shift < devices:
        came = lax.ppermute(reach, "tm", [(i, i + shift) for i in range(devices - shift)])
        join = lambda later: jnp.concatenate(
            [later[:size] + gain(later) * came[:size], later[size:] * came[size:]], axis=0
        )
        before = came if before is None else join(before)
        reach = join(reach)
        shift *= 2
    if before is None:
        return jnp.zeros_like(own[:size])
    return before[:size]


def shards(devices, signal, entry_map, readout, gate_input, log_decay, norm_gain):
    heads, length = log_decay.shape
    width = signal.shape[1]
    head_size = width // heads
    state_size = entry_map.shape[1]
    split = devices == 4 and width % 256 == 0
    tile = 512
    decay = log_decay
    if heads < HEAD_ROWS:
        decay = jnp.pad(log_decay, ((0, HEAD_ROWS - heads), (0, 0)))
    place = lax.axis_index("tm").astype(jnp.int32).reshape(1)
    made = local_states(place, decay, entry_map, signal, head_size, split, tile)
    start = jnp.zeros((state_size, width), F32)
    common = (decay, entry_map, readout, signal, gate_input)
    inside, share, state = local_part(0, 2, *common, start, None, head_size, tile)
    if split:
        own, first, second = made
        one = lax.ppermute(first, "tm", [(0, 1), (1, 2)])
        two = lax.ppermute(second, "tm", [(2, 1), (0, 2)])
        first, second, kept = blend(place, one, two, own)
        one = lax.ppermute(first, "tm", [(1, 2), (2, 3)])
        two = lax.ppermute(second, "tm", [(1, 3), (2, 1)])
        incoming = (one, two, kept)
    else:
        incoming = (scan_devices(made[0], devices),)
    inside, share, state = local_part(1, 2, *common, state, (inside, share), head_size, tile)
    return final_part(
        place, incoming, readout, inside, share, norm_gain.reshape(1, width), head_size, split, tile
    )


def solution(mesh):
    in_specs = (
        P(("parts", "tm"), ("head", "sub")),
        P(("parts", "tm"), None),
        P(("parts", "tm"), None),
        P(("parts", "tm"), ("head", "sub")),
        P(("head", "sub"), ("parts", "tm")),
        P(("head", "sub")),
    )
    out_specs = P(("parts", "tm"), ("head", "sub"))
    body = functools.partial(shards, mesh.shape["tm"])
    return jax.shard_map(body, mesh=mesh, in_specs=in_specs, out_specs=out_specs, check_vma=False)
```

```python
import functools

import jax
import jax.numpy as jnp
from jax import lax
from jax.experimental import pallas as pl
from jax.experimental.pallas import tpu as pltpu
from jax.sharding import PartitionSpec as P

CHUNK = 128
HEAD_ROWS = 8
EPSILON = 1e-05
F32 = jnp.float32
BF16 = jnp.bfloat16
TN = (((0,), (0,)), ((), ()))
NT = (((1,), (1,)), ((), ()))
IN_HBM = pl.BlockSpec(memory_space=pltpu.HBM)
IN_VMEM = pl.BlockSpec(memory_space=pltpu.VMEM)


def mm(left, right, dims=(((1,), (0,)), ((), ()))):
    return lax.dot_general(left, right, dims, preferred_element_type=F32)


def two_terms(value):
    high = value.astype(BF16)
    return high, (value - high.astype(F32)).astype(BF16)


def spread_matrix(width, head_size):
    row = lax.broadcasted_iota(jnp.int32, (2 * HEAD_ROWS, width), 0)
    column = lax.broadcasted_iota(jnp.int32, (2 * HEAD_ROWS, width), 1)
    own = lax.rem(row, HEAD_ROWS) == lax.div(column, head_size)
    return own.astype(F32).astype(BF16)


def stacked(decay):
    chunks = decay.shape[1] // CHUNK
    return jnp.concatenate([decay[:, c * CHUNK : (c + 1) * CHUNK] for c in range(chunks)], axis=0)


def sums(decay_rows, matrix):
    high = decay_rows.astype(BF16)
    rest = decay_rows - high.astype(F32)
    middle = rest.astype(BF16)
    low = (rest - middle.astype(F32)).astype(BF16)
    return mm(high, matrix) + (mm(middle, matrix) + mm(low, matrix))


def pair_rows(value):
    high, low = two_terms(value)
    return jnp.concatenate([high, low], axis=0)


def indicator(test):
    return test.astype(F32).astype(BF16)


def copy_rows(source, target, semaphore, start, rows):
    where = pl.ds(start, rows)
    return pltpu.make_async_copy(source.at[where], target.at[where], semaphore)


def state_kernel(split, head_size, pieces, place_ref, decay_hbm, entry_hbm, signal_hbm, *rest):
    outs, (entry_ref, signal_ref, decay_ref, factor_ref, semaphores) = rest[:-5], rest[-5:]
    length, width = signal_ref.shape
    rows = length // pieces
    chunks = length // CHUNK
    decay_copy = pltpu.make_async_copy(decay_hbm, decay_ref, semaphores.at[2 * pieces])
    decay_copy.start()
    copies = []
    for k in range(pieces):
        copies.append(copy_rows(entry_hbm, entry_ref, semaphores.at[k], k * rows, rows))
        copies.append(copy_rows(signal_hbm, signal_ref, semaphores.at[pieces + k], k * rows, rows))
    for copy in copies:
        copy.start()
    spread = spread_matrix(width, head_size)
    decay_copy.wait()
    tall = stacked(decay_ref[...])
    s_from = lax.broadcasted_iota(jnp.int32, (CHUNK, 2 * CHUNK), 0)
    s_to = lax.broadcasted_iota(jnp.int32, (CHUNK, 2 * CHUNK), 1)
    both = sums(tall, indicator((s_from > s_to) | (s_to >= CHUNK)))
    later = jnp.zeros((HEAD_ROWS, CHUNK), F32)
    for c in reversed(range(chunks)):
        part = both[c * HEAD_ROWS : (c + 1) * HEAD_ROWS]
        factor_ref[c] = pair_rows(jnp.exp(part[:, :CHUNK] + later))
        later = later + part[:, CHUNK:]
    gain = mm(pair_rows(jnp.exp(later[:, :HEAD_ROWS])), spread, TN)
    states = None
    for k in range(pieces):
        copies[2 * k].wait()
        copies[2 * k + 1].wait()
        for start in range(k * rows, (k + 1) * rows, 2 * CHUNK):
            where = pl.ds(start, 2 * CHUNK)
            c = start // CHUNK
            factor = jnp.concatenate([mm(factor_ref[c + j], spread, TN) for j in range(2)], axis=0)
            scaled = (signal_ref[where, :].astype(F32) * factor).astype(BF16)
            term = mm(entry_ref[where, :], scaled, TN)
            states = term if states is None else states + term
    size = states.shape[0]
    if split:
        own_ref, first_ref, second_ref = outs
        half = width // 2
        for k in range(2):
            own_ref[k, :size, :] = states[:, k * half : (k + 1) * half]
            own_ref[k, size:, :] = gain[:, k * half : (k + 1) * half]

        @pl.when(place_ref[0] == 0)
        def _():
            first_ref[...] = own_ref[0]
            second_ref[...] = own_ref[1]

        @pl.when(place_ref[0] != 0)
        def _():
            first_ref[...] = own_ref[1]
            second_ref[...] = own_ref[0]
    else:
        (own_ref,) = outs
        own_ref[:size, :] = states
        own_ref[size:, :] = gain


def local_states(place, decay, entry_map, signal, head_size, split, pieces):
    length, width = signal.shape
    state_size = entry_map.shape[1]
    tall = state_size + HEAD_ROWS
    if split:
        shapes = [(2, tall, width // 2), (tall, width // 2), (tall, width // 2)]
    else:
        shapes = [(tall, width)]
    return pl.pallas_call(
        functools.partial(state_kernel, split, head_size, pieces),
        in_specs=[pl.BlockSpec(memory_space=pltpu.SMEM)] + [IN_HBM] * 3,
        out_specs=[IN_VMEM] * (len(shapes) + 2),
        out_shape=[pltpu.VMEM(s, F32) for s in shapes]
        + [pltpu.VMEM((length, state_size), BF16), pltpu.VMEM((length, width), BF16)],
        scratch_shapes=[
            pltpu.VMEM((HEAD_ROWS, length), F32),
            pltpu.VMEM((length // CHUNK, 2 * HEAD_ROWS, CHUNK), BF16),
            pltpu.SemaphoreType.DMA((2 * pieces + 1,)),
        ],
        name="device_states",
        compiler_params=pltpu.CompilerParams(vmem_limit_bytes=16 << 20),
        cost_estimate=pl.CostEstimate(
            flops=2 * length * width * state_size,
            bytes_accessed=2 * length * (width + state_size),
            transcendentals=0,
        ),
    )(place, decay, entry_map, signal)


def local_kernel(base, head_size, pieces, decay_hbm, readout_hbm, gate_hbm, gain_hbm, entry_ref, signal_ref, state_in, *rest):
    inside_ref, share_ref, readout_ref, gain_ref, state_ref = rest[:5]
    decay_ref, gate_ref, in_ref, out_ref, whole_ref, step_ref, semaphores = rest[5:]
    length, width = signal_ref.shape
    part_rows = inside_ref.shape[0]
    rows = part_rows // pieces
    chunks = length // CHUNK
    decay_copy = pltpu.make_async_copy(decay_hbm, decay_ref, semaphores.at[0])
    readout_copy = pltpu.make_async_copy(readout_hbm.at[pl.ds(base, part_rows)], readout_ref, semaphores.at[1])
    gain_copy = pltpu.make_async_copy(gain_hbm, gain_ref, semaphores.at[2])
    gate_copies = [
        pltpu.make_async_copy(
            gate_hbm.at[pl.ds(base + k * rows, rows)], gate_ref.at[pl.ds(k * rows, rows)], semaphores.at[3 + k]
        )
        for k in range(pieces)
    ]
    decay_copy.start()
    readout_copy.start()
    for copy in gate_copies:
        copy.start()
    gain_copy.start()
    spread = spread_matrix(width, head_size)
    decay_copy.wait()
    tall = stacked(decay_ref[...])
    half = CHUNK // 2
    s_from = lax.broadcasted_iota(jnp.int32, (CHUNK, CHUNK), 0)
    s_to = lax.broadcasted_iota(jnp.int32, (CHUNK, CHUNK), 1)
    early = (s_from < half).astype(F32)
    centred = ((s_from <= s_to).astype(F32) - early).astype(BF16)
    matrix = jnp.concatenate([centred, early.astype(BF16), (1.0 - early).astype(BF16)], axis=1)
    three = sums(tall, matrix)
    before = jnp.zeros((HEAD_ROWS, CHUNK), F32)
    for c in range(chunks):
        part = three[c * HEAD_ROWS : (c + 1) * HEAD_ROWS]
        from_middle = part[:, :CHUNK]
        to_middle = part[:, CHUNK : 2 * CHUNK]
        onward = part[:, 2 * CHUNK :]
        if base <= c * CHUNK < base + part_rows:
            in_ref[c] = pair_rows(jnp.exp(-from_middle))
            out_ref[c] = pair_rows(jnp.exp(from_middle))
            whole_ref[c] = pair_rows(jnp.exp(before + (to_middle + from_middle)))
            if c + 1 < chunks:
                following = three[(c + 1) * HEAD_ROWS : (c + 2) * HEAD_ROWS, CHUNK : 2 * CHUNK]
                step_ref[c] = pair_rows(jnp.exp(onward + following))
            else:
                step_ref[c] = pair_rows(jnp.exp(onward))
        before = before + (to_middle + onward)
    t_row = lax.broadcasted_iota(jnp.int32, (CHUNK, CHUNK), 0)
    s_column = lax.broadcasted_iota(jnp.int32, (CHUNK, CHUNK), 1)
    causal = t_row >= s_column
    state = state_in[...] if base else jnp.zeros(state_ref.shape, F32)
    readout_copy.wait()
    for k in range(part_rows // CHUNK):
        if k % (rows // CHUNK) == 0:
            gate_copies[k // (rows // CHUNK)].wait()
        c = base // CHUNK + k
        here = pl.ds(k * CHUNK, CHUNK)
        where = pl.ds(c * CHUNK, CHUNK)
        entry = entry_ref[where, :]
        readout = readout_ref[here, :]
        scaled = (signal_ref[where, :].astype(F32) * mm(in_ref[c], spread, TN)).astype(BF16)
        scores = jnp.where(causal, mm(readout, entry, NT), 0.0).astype(BF16)
        left = jnp.concatenate([scores, readout], axis=1)
        right = jnp.concatenate([scaled, state.astype(BF16)], axis=0)
        output = mm(left, right) * mm(out_ref[c], spread, TN)
        state = state + mm(entry, scaled, TN)
        onward = mm(step_ref[c][:, :HEAD_ROWS], spread, TN)
        size = state.shape[0]
        state = (state.reshape(size // HEAD_ROWS, HEAD_ROWS, width) * onward[None]).reshape(size, width)
        gate = gate_ref[here, :].astype(F32)
        silu = gate / (1.0 + jnp.exp(-gate))
        inside_ref[here, :] = (output * silu).astype(BF16)
        share_ref[here, :] = (silu * mm(whole_ref[c], spread, TN)).astype(BF16)
    state_ref[...] = state
    gain_copy.wait()


def local_part(index, parts, decay, readout, gate_input, norm_gain, entry_map, signal, state, head_size, pieces):
    length, width = signal.shape
    state_size = entry_map.shape[1]
    rows = length // parts
    chunks = length // CHUNK
    return pl.pallas_call(
        functools.partial(local_kernel, index * rows, head_size, pieces),
        in_specs=[IN_HBM] * 4 + [IN_VMEM] * 3,
        out_specs=[IN_VMEM] * 5,
        out_shape=[
            pltpu.VMEM((rows, width), BF16),
            pltpu.VMEM((rows, width), BF16),
            pltpu.VMEM((rows, state_size), BF16),
            pltpu.VMEM((1, width), F32),
            pltpu.VMEM((state_size, width), F32),
        ],
        scratch_shapes=[pltpu.VMEM((HEAD_ROWS, length), F32), pltpu.VMEM((rows, width), BF16)]
        + [pltpu.VMEM((chunks, 2 * HEAD_ROWS, CHUNK), BF16)] * 4
        + [pltpu.SemaphoreType.DMA((3 + pieces,))],
        name="local_part",
        compiler_params=pltpu.CompilerParams(vmem_limit_bytes=16 << 20),
        cost_estimate=pl.CostEstimate(
            flops=8 * length * width * state_size // parts,
            bytes_accessed=2 * length * (4 * width + 2 * state_size) // parts,
            transcendentals=length * width // parts,
        ),
    )(decay, readout, gate_input, norm_gain, entry_map, signal, state)


def final_kernel(split, head_size, parts, rows, place_ref, *rest):
    count = 3 if split else 1
    incoming, rest = rest[:count], rest[count:]
    groups = [rest[3 * p : 3 * p + 3] for p in range(parts)]
    gain_ref, result_hbm, result_ref, terms_ref, semaphores = rest[3 * parts :]
    size = groups[0][0].shape[1]
    part_rows, width = groups[0][1].shape

    def keep(value, at):
        high, low = two_terms(value)
        terms_ref[:size, at : at + value.shape[1]] = high
        terms_ref[size:, at : at + value.shape[1]] = low

    if split:
        one, two, kept = incoming
        place = place_ref[0]
        half = width // 2

        @pl.when(place == 1)
        def _():
            keep(kept[...], 0)
            keep(two[...], half)

        @pl.when(place == 2)
        def _():
            keep(one[...], 0)
            keep(kept[...], half)

        @pl.when((place != 1) & (place != 2))
        def _():
            keep(two[...], 0)
            keep(one[...], half)
    else:
        keep(incoming[0][...], 0)

    group = min(width, 256)
    row = lax.broadcasted_iota(jnp.int32, (group, group), 0)
    column = lax.broadcasted_iota(jnp.int32, (group, group), 1)
    same = lax.div(row, head_size) == lax.div(column, head_size)
    average = jnp.where(same, 1.0 / head_size, 0.0).astype(BF16)
    gain = gain_ref[...]
    copies = []
    for p, (readout_ref, inside_ref, share_ref) in enumerate(groups):
        for start in range(0, part_rows, rows):
            where = pl.ds(start, rows)
            there = pl.ds(p * part_rows + start, rows)
            readout = readout_ref[where, :]
            across = mm(jnp.concatenate([readout, readout], axis=1), terms_ref[...])
            gated = inside_ref[where, :].astype(F32) + share_ref[where, :].astype(F32) * across
            squares = (gated * gated).astype(BF16)
            mean = jnp.concatenate(
                [mm(squares[:, g : g + group], average) for g in range(0, width, group)], axis=1
            )
            result_ref[there, :] = (gated * lax.rsqrt(mean + EPSILON) * gain).astype(BF16)
            copy = pltpu.make_async_copy(result_ref.at[there], result_hbm.at[there], semaphores.at[len(copies)])
            copy.start()
            copies.append(copy)
    for copy in copies:
        copy.wait()


def final_part(place, incoming, groups, norm_gain, head_size, split, rows):
    part_rows, width = groups[0][1].shape
    length = part_rows * len(groups)
    state_size = groups[0][0].shape[1]
    return pl.pallas_call(
        functools.partial(final_kernel, split, head_size, len(groups), rows),
        in_specs=[pl.BlockSpec(memory_space=pltpu.SMEM)]
        + [IN_VMEM] * (len(incoming) + 3 * len(groups) + 1),
        out_specs=IN_HBM,
        out_shape=jax.ShapeDtypeStruct((length, width), BF16),
        scratch_shapes=[
            pltpu.VMEM((length, width), BF16),
            pltpu.VMEM((2 * state_size, width), BF16),
            pltpu.SemaphoreType.DMA((length // rows,)),
        ],
        name="final_part",
        compiler_params=pltpu.CompilerParams(vmem_limit_bytes=16 << 20),
        cost_estimate=pl.CostEstimate(
            flops=4 * length * width * state_size,
            bytes_accessed=2 * length * (3 * width + state_size),
            transcendentals=length * width,
        ),
    )(place, *incoming, *[v for g in groups for v in g], norm_gain)


def blend_kernel(place_ref, one_ref, two_ref, own_ref, first_ref, second_ref, kept_ref):
    size = kept_ref.shape[0]
    width = kept_ref.shape[1]

    def scaled(rows_ref, value):
        gain = rows_ref[size:, :]
        shape = (size // HEAD_ROWS, HEAD_ROWS, width)
        return (value.reshape(shape) * gain[None]).reshape(size, width)

    @pl.when(place_ref[0] == 1)
    def _():
        mine = own_ref.at[0]
        first = one_ref[:size, :]
        second = mine[:size, :] + scaled(mine, first)
        first_ref[...] = second
        second_ref[...] = two_ref[:size, :] + scaled(two_ref, second)
        kept_ref[...] = first

    @pl.when(place_ref[0] != 1)
    def _():
        mine = own_ref.at[1]
        first = two_ref[:size, :]
        second = one_ref[:size, :] + scaled(one_ref, first)
        first_ref[...] = mine[:size, :] + scaled(mine, second)
        second_ref[...] = first
        kept_ref[...] = second


def blend(place, one, two, own):
    size = one.shape[0] - HEAD_ROWS
    width = one.shape[1]
    return pl.pallas_call(
        blend_kernel,
        in_specs=[pl.BlockSpec(memory_space=pltpu.SMEM)] + [IN_VMEM] * 3,
        out_specs=[IN_VMEM] * 3,
        out_shape=[pltpu.VMEM((size, width), F32)] * 3,
        name="blend",
        compiler_params=pltpu.CompilerParams(vmem_limit_bytes=4 << 20),
    )(place, one, two, own)


def scan_devices(own, devices):
    size = own.shape[0] - HEAD_ROWS
    gain = lambda v: v[size : size + 1]
    reach, before = own, None
    shift = 1
    while shift < devices:
        came = lax.ppermute(reach, "tm", [(i, i + shift) for i in range(devices - shift)])
        join = lambda later: jnp.concatenate(
            [later[:size] + gain(later) * came[:size], later[size:] * came[size:]], axis=0
        )
        before = came if before is None else join(before)
        reach = join(reach)
        shift *= 2
    if before is None:
        return jnp.zeros_like(own[:size])
    return before[:size]


def shards(devices, signal, entry_map, readout, gate_input, log_decay, norm_gain):
    heads, length = log_decay.shape
    width = signal.shape[1]
    head_size = width // heads
    split = devices == 4 and width % 256 == 0
    decay = log_decay
    if heads < HEAD_ROWS:
        decay = jnp.pad(log_decay, ((0, HEAD_ROWS - heads), (0, 0)))
    place = lax.axis_index("tm").astype(jnp.int32).reshape(1)
    *made, entry_map, signal = local_states(place, decay, entry_map, signal, head_size, split, 4)
    common = (decay, readout, gate_input, norm_gain.reshape(1, width), entry_map, signal)
    nothing = jnp.zeros((8, 128), F32)
    if split:
        own, first, second = made
        one = lax.ppermute(first, "tm", [(0, 1), (1, 2)])
        two = lax.ppermute(second, "tm", [(2, 1), (0, 2)])
    inside_a, share_a, readout_a, _, state = local_part(0, 2, *common, nothing, head_size, 2)
    if split:
        one, two, state = lax.optimization_barrier((one, two, state))
        first, second, kept = blend(place, one, two, own)
        one = lax.ppermute(first, "tm", [(1, 2), (2, 3)])
        two = lax.ppermute(second, "tm", [(1, 3), (2, 1)])
        incoming = (one, two, kept)
    else:
        incoming = (scan_devices(made[0], devices),)
    inside_b, share_b, readout_b, gain, _ = local_part(1, 2, *common, state, head_size, 2)
    groups = ((readout_a, inside_a, share_a), (readout_b, inside_b, share_b))
    return final_part(place, incoming, groups, gain, head_size, split, 512)


def solution(mesh):
    in_specs = (
        P(("parts", "tm"), ("head", "sub")),
        P(("parts", "tm"), None),
        P(("parts", "tm"), None),
        P(("parts", "tm"), ("head", "sub")),
        P(("head", "sub"), ("parts", "tm")),
        P(("head", "sub")),
    )
    out_specs = P(("parts", "tm"), ("head", "sub"))
    body = functools.partial(shards, mesh.shape["tm"])
    return jax.shard_map(body, mesh=mesh, in_specs=in_specs, out_specs=out_specs, check_vma=False)
```

```python
import functools

import jax
import jax.numpy as jnp
from jax import lax
from jax.experimental import pallas as pl
from jax.experimental.pallas import tpu as pltpu
from jax.sharding import PartitionSpec as P

CHUNK = 128
HEAD_ROWS = 8
EPSILON = 1e-05
F32 = jnp.float32
BF16 = jnp.bfloat16
TN = (((0,), (0,)), ((), ()))
NT = (((1,), (1,)), ((), ()))
IN_HBM = pl.BlockSpec(memory_space=pltpu.HBM)
IN_VMEM = pl.BlockSpec(memory_space=pltpu.VMEM)


def mm(left, right, dims=(((1,), (0,)), ((), ()))):
    return lax.dot_general(left, right, dims, preferred_element_type=F32)


def two_terms(value):
    high = value.astype(BF16)
    return high, (value - high.astype(F32)).astype(BF16)


def spread_matrix(width, head_size):
    row = lax.broadcasted_iota(jnp.int32, (2 * HEAD_ROWS, width), 0)
    column = lax.broadcasted_iota(jnp.int32, (2 * HEAD_ROWS, width), 1)
    own = lax.rem(row, HEAD_ROWS) == lax.div(column, head_size)
    return own.astype(F32).astype(BF16)


def stacked(decay):
    chunks = decay.shape[1] // CHUNK
    return jnp.concatenate([decay[:, c * CHUNK : (c + 1) * CHUNK] for c in range(chunks)], axis=0)


def sums(decay_rows, matrix):
    high = decay_rows.astype(BF16)
    rest = decay_rows - high.astype(F32)
    middle = rest.astype(BF16)
    low = (rest - middle.astype(F32)).astype(BF16)
    return mm(high, matrix) + (mm(middle, matrix) + mm(low, matrix))


def pair_rows(value):
    high, low = two_terms(value)
    return jnp.concatenate([high, low], axis=0)


def indicator(test):
    return test.astype(F32).astype(BF16)


def spread_rows(factor_ref, chunks, spread):
    return jnp.concatenate([mm(factor_ref[c], spread, TN) for c in chunks], axis=0)


def copy_rows(source, target, semaphore, start, rows):
    where = pl.ds(start, rows)
    return pltpu.make_async_copy(source.at[where], target.at[where], semaphore)


def state_kernel(split, head_size, pieces, place_ref, decay_hbm, entry_hbm, signal_hbm, *rest):
    outs, (entry_ref, signal_ref, decay_ref, factor_ref, semaphores) = rest[:-5], rest[-5:]
    length, width = signal_ref.shape
    rows = length // pieces
    chunks = length // CHUNK
    decay_copy = pltpu.make_async_copy(decay_hbm, decay_ref, semaphores.at[2 * pieces])
    decay_copy.start()
    copies = []
    for k in range(pieces):
        copies.append(copy_rows(entry_hbm, entry_ref, semaphores.at[k], k * rows, rows))
        copies.append(copy_rows(signal_hbm, signal_ref, semaphores.at[pieces + k], k * rows, rows))
    for copy in copies:
        copy.start()
    spread = spread_matrix(width, head_size)
    decay_copy.wait()
    tall = stacked(decay_ref[...])
    s_from = lax.broadcasted_iota(jnp.int32, (CHUNK, 2 * CHUNK), 0)
    s_to = lax.broadcasted_iota(jnp.int32, (CHUNK, 2 * CHUNK), 1)
    both = sums(tall, indicator((s_from > s_to) | (s_to >= CHUNK)))
    later = jnp.zeros((HEAD_ROWS, CHUNK), F32)
    for c in reversed(range(chunks)):
        part = both[c * HEAD_ROWS : (c + 1) * HEAD_ROWS]
        factor_ref[c] = pair_rows(jnp.exp(part[:, :CHUNK] + later))
        later = later + part[:, CHUNK:]
    gain = mm(pair_rows(jnp.exp(later[:, :HEAD_ROWS])), spread, TN)
    states = None
    for k in range(pieces):
        copies[2 * k].wait()
        copies[2 * k + 1].wait()
        where = pl.ds(k * rows, rows)
        here = range(k * rows // CHUNK, (k + 1) * rows // CHUNK)
        scaled = (signal_ref[where, :].astype(F32) * spread_rows(factor_ref, here, spread)).astype(BF16)
        term = mm(entry_ref[where, :], scaled, TN)
        states = term if states is None else states + term
    size = states.shape[0]
    if split:
        own_ref, first_ref, second_ref = outs
        half = width // 2
        for k in range(2):
            own_ref[k, :size, :] = states[:, k * half : (k + 1) * half]
            own_ref[k, size:, :] = gain[:, k * half : (k + 1) * half]

        @pl.when(place_ref[0] == 0)
        def _():
            first_ref[...] = own_ref[0]
            second_ref[...] = own_ref[1]

        @pl.when(place_ref[0] != 0)
        def _():
            first_ref[...] = own_ref[1]
            second_ref[...] = own_ref[0]
    else:
        (own_ref,) = outs
        own_ref[:size, :] = states
        own_ref[size:, :] = gain


def local_states(place, decay, entry_map, signal, head_size, split, pieces):
    length, width = signal.shape
    state_size = entry_map.shape[1]
    tall = state_size + HEAD_ROWS
    if split:
        shapes = [(2, tall, width // 2), (tall, width // 2), (tall, width // 2)]
    else:
        shapes = [(tall, width)]
    return pl.pallas_call(
        functools.partial(state_kernel, split, head_size, pieces),
        in_specs=[pl.BlockSpec(memory_space=pltpu.SMEM)] + [IN_HBM] * 3,
        out_specs=[IN_VMEM] * (len(shapes) + 2),
        out_shape=[pltpu.VMEM(s, F32) for s in shapes]
        + [pltpu.VMEM((length, state_size), BF16), pltpu.VMEM((length, width), BF16)],
        scratch_shapes=[
            pltpu.VMEM((HEAD_ROWS, length), F32),
            pltpu.VMEM((length // CHUNK, 2 * HEAD_ROWS, CHUNK), BF16),
            pltpu.SemaphoreType.DMA((2 * pieces + 1,)),
        ],
        name="device_states",
        compiler_params=pltpu.CompilerParams(vmem_limit_bytes=56 << 20),
        cost_estimate=pl.CostEstimate(
            flops=2 * length * width * state_size,
            bytes_accessed=2 * length * (width + state_size),
            transcendentals=0,
        ),
    )(place, decay, entry_map, signal)


def by_head(value, factor):
    rows, width = value.shape
    return (value.reshape(rows // HEAD_ROWS, HEAD_ROWS, width) * factor[None]).reshape(rows, width)


def local_kernel(base, head_size, group, decay_ref, readout_ref, gate_ref, entry_ref, signal_ref, state_in, *rest):
    inside_ref, share_ref, state_ref, in_ref, out_ref = rest
    length, width = signal_ref.shape
    sides, part_rows, side = inside_ref.shape
    first = base // CHUNK
    many = part_rows // CHUNK
    spread = spread_matrix(width, head_size)
    tall = stacked(decay_ref[...])
    half = CHUNK // 2
    s_from = lax.broadcasted_iota(jnp.int32, (CHUNK, CHUNK), 0)
    s_to = lax.broadcasted_iota(jnp.int32, (CHUNK, CHUNK), 1)
    early = (s_from < half).astype(F32)
    centred = ((s_from <= s_to).astype(F32) - early).astype(BF16)
    matrix = jnp.concatenate([centred, early.astype(BF16), (1.0 - early).astype(BF16)], axis=1)
    three = sums(tall, matrix)
    before = jnp.zeros((HEAD_ROWS, HEAD_ROWS), F32)
    to_here, to_next = [], []
    for c in range(first + many):
        part = three[c * HEAD_ROWS : (c + 1) * HEAD_ROWS]
        to_middle = part[:, CHUNK : CHUNK + HEAD_ROWS]
        onward = part[:, 2 * CHUNK : 2 * CHUNK + HEAD_ROWS]
        if c >= first:
            from_middle = part[:, :CHUNK]
            in_ref[c - first] = pair_rows(jnp.exp(-from_middle))
            out_ref[c - first] = pair_rows(jnp.exp(from_middle))
            to_here.append(pair_rows(jnp.exp(before + to_middle)))
            if (c + 1) * CHUNK < length:
                following = three[(c + 1) * HEAD_ROWS : (c + 2) * HEAD_ROWS, CHUNK : CHUNK + HEAD_ROWS]
                to_next.append(pair_rows(jnp.exp(onward + following)))
            else:
                to_next.append(pair_rows(jnp.exp(onward)))
        before = before + (to_middle + onward)
    causal = s_from >= s_to
    state = state_in[...] if base else jnp.zeros(state_ref.shape, F32)
    for start in range(0, many, group):
        here = range(start, start + group)
        where = pl.ds(base + start * CHUNK, group * CHUNK)
        there = pl.ds(start * CHUNK, group * CHUNK)
        cut = lambda value, j: value[j * CHUNK : (j + 1) * CHUNK]
        entry = entry_ref[where, :]
        readout = readout_ref[where, :]
        scaled = (signal_ref[where, :].astype(F32) * spread_rows(in_ref, here, spread)).astype(BF16)
        scores, added, passed = [], [], []
        for j in range(group):
            products = mm(cut(readout, j), cut(entry, j), NT)
            scores.append(jnp.where(causal, products, 0.0).astype(BF16))
            added.append(mm(cut(entry, j), cut(scaled, j), TN))
        for j in range(group):
            passed.append(state.astype(BF16))
            state = by_head(state + added[j], mm(to_next[start + j], spread, TN))
        output = jnp.concatenate(
            [
                mm(
                    jnp.concatenate([scores[j], cut(readout, j)], axis=1),
                    jnp.concatenate([cut(scaled, j), passed[j]], axis=0),
                )
                for j in range(group)
            ],
            axis=0,
        )
        gate = gate_ref[where, :].astype(F32)
        opened = gate / (1.0 + jnp.exp(-gate)) * spread_rows(out_ref, here, spread)
        inside = (output * opened).astype(BF16)
        share = jnp.concatenate(
            [by_head(cut(opened, j), mm(to_here[start + j], spread, TN)) for j in range(group)], axis=0
        ).astype(BF16)
        for k in range(sides):
            inside_ref[k, there, :] = inside[:, k * side : (k + 1) * side]
            share_ref[k, there, :] = share[:, k * side : (k + 1) * side]
    state_ref[...] = state


def local_part(index, parts, decay, readout, gate_input, entry_map, signal, state, head_size, sides, group):
    length, width = signal.shape
    state_size = entry_map.shape[1]
    rows = length // parts
    return pl.pallas_call(
        functools.partial(local_kernel, index * rows, head_size, group),
        in_specs=[IN_VMEM] * 6,
        out_specs=[IN_VMEM] * 3,
        out_shape=[pltpu.VMEM((sides, rows, width // sides), BF16)] * 2 + [pltpu.VMEM((state_size, width), F32)],
        scratch_shapes=[pltpu.VMEM((rows // CHUNK, 2 * HEAD_ROWS, CHUNK), BF16)] * 2,
        name="local_part",
        compiler_params=pltpu.CompilerParams(vmem_limit_bytes=16 << 20),
        cost_estimate=pl.CostEstimate(
            flops=8 * length * width * state_size // parts,
            bytes_accessed=2 * length * (4 * width + 2 * state_size) // parts,
            transcendentals=length * width // parts,
        ),
    )(decay, readout, gate_input, entry_map, signal, state)


def final_kernel(turn, head_size, parts, rows, place_ref, *rest):
    count = 1 if turn is None else 2
    incoming, rest = rest[:count], rest[count:]
    readout_ref, gain_ref, *rest = rest
    groups, rest = [rest[2 * p : 2 * p + 2] for p in range(parts)], rest[2 * parts :]
    result_hbm, result_ref, terms_ref, semaphores = rest[-4:]
    size = readout_ref.shape[1]
    _, part_rows, width = groups[0][0].shape

    def keep(value):
        high, low = two_terms(value)
        terms_ref[:size, :] = high
        terms_ref[size:, :] = low

    if turn is None:
        side = 0
        keep(incoming[0][...])
    else:
        place = place_ref[0]
        side = jnp.where(place == 1, turn, 1 - turn)
        other = (place == 1) | (place == 2) if turn == 0 else place == 2

        @pl.when(other)
        def _():
            keep(incoming[0][...])

        @pl.when(jnp.logical_not(other))
        def _():
            keep(incoming[1][...])

    group = min(width, 256)
    row = lax.broadcasted_iota(jnp.int32, (group, group), 0)
    column = lax.broadcasted_iota(jnp.int32, (group, group), 1)
    same = lax.div(row, head_size) == lax.div(column, head_size)
    average = jnp.where(same, 1.0 / head_size, 0.0).astype(BF16)
    gain = gain_ref[side]
    terms = terms_ref[...]
    columns = pl.ds(0, width) if turn is None else pl.ds(pl.multiple_of(side * width, width), width)
    copies = []
    for p, (inside_ref, share_ref) in enumerate(groups):
        for start in range(0, part_rows, rows):
            where = pl.ds(start, rows)
            there = pl.ds(p * part_rows + start, rows)
            readout = readout_ref[there, :]
            across = mm(jnp.concatenate([readout, readout], axis=1), terms)
            gated = inside_ref[side, where, :].astype(F32) + share_ref[side, where, :].astype(F32) * across
            squares = (gated * gated).astype(BF16)
            mean = jnp.concatenate(
                [mm(squares[:, g : g + group], average) for g in range(0, width, group)], axis=1
            )
            result_ref[there, :] = (gated * lax.rsqrt(mean + EPSILON) * gain).astype(BF16)
            copy = pltpu.make_async_copy(
                result_ref.at[there], result_hbm.at[there, columns], semaphores.at[len(copies)]
            )
            copy.start()
            copies.append(copy)
    for copy in copies:
        copy.wait()


def final_part(turn, place, incoming, readout, norm_gain, groups, kept, head_size, rows):
    sides, part_rows, width = groups[0][0].shape
    length = part_rows * len(groups)
    state_size = readout.shape[1]
    arguments = [place, *incoming, readout, norm_gain, *[v for g in groups for v in g]]
    in_specs = [pl.BlockSpec(memory_space=pltpu.SMEM)] + [IN_VMEM] * (len(arguments) - 1)
    aliases = {}
    if kept is not None:
        aliases = {len(arguments): 0}
        arguments.append(kept)
        in_specs.append(IN_HBM)
    return pl.pallas_call(
        functools.partial(final_kernel, turn, head_size, len(groups), rows),
        in_specs=in_specs,
        out_specs=IN_HBM,
        out_shape=jax.ShapeDtypeStruct((length, width * sides), BF16),
        input_output_aliases=aliases,
        scratch_shapes=[
            pltpu.VMEM((length, width), BF16),
            pltpu.VMEM((2 * state_size, width), BF16),
            pltpu.SemaphoreType.DMA((length // rows,)),
        ],
        name="final_part",
        compiler_params=pltpu.CompilerParams(vmem_limit_bytes=16 << 20),
        cost_estimate=pl.CostEstimate(
            flops=4 * length * width * state_size,
            bytes_accessed=2 * length * (3 * width + state_size),
            transcendentals=length * width,
        ),
    )(*arguments)


def blend_kernel(place_ref, one_ref, two_ref, own_ref, first_ref, second_ref, kept_ref):
    size = kept_ref.shape[0]
    width = kept_ref.shape[1]

    def scaled(rows_ref, value):
        gain = rows_ref[size:, :]
        shape = (size // HEAD_ROWS, HEAD_ROWS, width)
        return (value.reshape(shape) * gain[None]).reshape(size, width)

    @pl.when(place_ref[0] == 1)
    def _():
        mine = own_ref.at[0]
        first = one_ref[:size, :]
        second = mine[:size, :] + scaled(mine, first)
        first_ref[...] = second
        second_ref[...] = two_ref[:size, :] + scaled(two_ref, second)
        kept_ref[...] = first

    @pl.when(place_ref[0] != 1)
    def _():
        mine = own_ref.at[1]
        first = two_ref[:size, :]
        second = one_ref[:size, :] + scaled(one_ref, first)
        first_ref[...] = mine[:size, :] + scaled(mine, second)
        second_ref[...] = first
        kept_ref[...] = second


def blend(place, one, two, own):
    size = one.shape[0] - HEAD_ROWS
    width = one.shape[1]
    return pl.pallas_call(
        blend_kernel,
        in_specs=[pl.BlockSpec(memory_space=pltpu.SMEM)] + [IN_VMEM] * 3,
        out_specs=[IN_VMEM] * 3,
        out_shape=[pltpu.VMEM((size, width), F32)] * 3,
        name="blend",
        compiler_params=pltpu.CompilerParams(vmem_limit_bytes=4 << 20),
    )(place, one, two, own)


def scan_devices(own, devices):
    size = own.shape[0] - HEAD_ROWS
    gain = lambda v: v[size : size + 1]
    reach, before = own, None
    shift = 1
    while shift < devices:
        came = lax.ppermute(reach, "tm", [(i, i + shift) for i in range(devices - shift)])
        join = lambda later: jnp.concatenate(
            [later[:size] + gain(later) * came[:size], later[size:] * came[size:]], axis=0
        )
        before = came if before is None else join(before)
        reach = join(reach)
        shift *= 2
    if before is None:
        return jnp.zeros_like(own[:size])
    return before[:size]


def shards(devices, signal, entry_map, readout, gate_input, log_decay, norm_gain):
    heads, length = log_decay.shape
    width = signal.shape[1]
    head_size = width // heads
    split = devices == 4 and width % 256 == 0
    sides = 2 if split else 1
    decay = log_decay
    if heads < HEAD_ROWS:
        decay = jnp.pad(log_decay, ((0, HEAD_ROWS - heads), (0, 0)))
    place = lax.axis_index("tm").astype(jnp.int32).reshape(1)
    *made, entry_map, signal = local_states(place, decay, entry_map, signal, head_size, split, 4)
    common = (decay, readout, gate_input, entry_map, signal)
    nothing = jnp.zeros((8, 128), F32)
    if split:
        own, first, second = made
        one = lax.ppermute(first, "tm", [(0, 1), (1, 2)])
        two = lax.ppermute(second, "tm", [(2, 1), (0, 2)])
    *before, state = local_part(0, 2, *common, nothing, head_size, sides, 4)
    if split:
        one, two, state = lax.optimization_barrier((one, two, state))
        first, second, kept = blend(place, one, two, own)
        one = lax.ppermute(first, "tm", [(1, 2), (2, 3)])
        two = lax.ppermute(second, "tm", [(1, 3), (2, 1)])
    else:
        total = scan_devices(made[0], devices)
    *after, _ = local_part(1, 2, *common, state, head_size, sides, 4)
    common = (readout, norm_gain.reshape(sides, 1, width // sides), (before, after))
    if split:
        result = final_part(0, place, (kept, one), *common, None, head_size, 1024)
        return final_part(1, place, (one, two), *common, result, head_size, 1024)
    return final_part(None, place, (total,), *common, None, head_size, 1024)


def solution(mesh):
    in_specs = (
        P(("parts", "tm"), ("head", "sub")),
        P(("parts", "tm"), None),
        P(("parts", "tm"), None),
        P(("parts", "tm"), ("head", "sub")),
        P(("head", "sub"), ("parts", "tm")),
        P(("head", "sub")),
    )
    out_specs = P(("parts", "tm"), ("head", "sub"))
    body = functools.partial(shards, mesh.shape["tm"])
    return jax.shard_map(body, mesh=mesh, in_specs=in_specs, out_specs=out_specs, check_vma=False)
```

```python
import functools

import jax
import jax.numpy as jnp
from jax import lax
from jax.experimental import pallas as pl
from jax.experimental.pallas import tpu as pltpu
from jax.sharding import PartitionSpec as P

CHUNK = 128
HEAD_ROWS = 8
EPSILON = 1e-05
F32 = jnp.float32
BF16 = jnp.bfloat16
TN = (((0,), (0,)), ((), ()))
NT = (((1,), (1,)), ((), ()))
IN_HBM = pl.BlockSpec(memory_space=pltpu.HBM)
IN_VMEM = pl.BlockSpec(memory_space=pltpu.VMEM)


def mm(left, right, dims=(((1,), (0,)), ((), ()))):
    return lax.dot_general(left, right, dims, preferred_element_type=F32)


def two_terms(value):
    high = value.astype(BF16)
    return high, (value - high.astype(F32)).astype(BF16)


def spread_matrix(width, head_size):
    row = lax.broadcasted_iota(jnp.int32, (2 * HEAD_ROWS, width), 0)
    column = lax.broadcasted_iota(jnp.int32, (2 * HEAD_ROWS, width), 1)
    own = lax.rem(row, HEAD_ROWS) == lax.div(column, head_size)
    return own.astype(F32).astype(BF16)


def stacked(decay):
    chunks = decay.shape[1] // CHUNK
    return jnp.concatenate([decay[:, c * CHUNK : (c + 1) * CHUNK] for c in range(chunks)], axis=0)


def sums(decay_rows, matrix):
    high = decay_rows.astype(BF16)
    rest = decay_rows - high.astype(F32)
    middle = rest.astype(BF16)
    low = (rest - middle.astype(F32)).astype(BF16)
    return mm(high, matrix) + (mm(middle, matrix) + mm(low, matrix))


def pair_rows(value):
    high, low = two_terms(value)
    return jnp.concatenate([high, low], axis=0)


def indicator(test):
    return test.astype(F32).astype(BF16)


def spread_rows(factor_ref, chunks, spread):
    return jnp.concatenate([mm(factor_ref[c], spread, TN) for c in chunks], axis=0)


def copy_rows(source, target, semaphore, start, rows):
    where = pl.ds(start, rows)
    return pltpu.make_async_copy(source.at[where], target.at[where], semaphore)


def state_kernel(split, head_size, pieces, place_ref, decay_hbm, entry_hbm, signal_hbm, gate_hbm, *rest):
    outs, (entry_ref, signal_ref, gate_ref, decay_ref, factor_ref, semaphores) = rest[:-6], rest[-6:]
    length, width = signal_ref.shape
    rows = length // pieces
    chunks = length // CHUNK
    decay_copy = pltpu.make_async_copy(decay_hbm, decay_ref, semaphores.at[2 * pieces])
    decay_copy.start()
    copies = []
    for k in range(pieces):
        copies.append(copy_rows(entry_hbm, entry_ref, semaphores.at[k], k * rows, rows))
        copies.append(copy_rows(signal_hbm, signal_ref, semaphores.at[pieces + k], k * rows, rows))
    for copy in copies:
        copy.start()
    gate_copy = pltpu.make_async_copy(
        gate_hbm.at[pl.ds(0, gate_ref.shape[0])], gate_ref, semaphores.at[2 * pieces + 1]
    )
    gate_copy.start()
    spread = spread_matrix(width, head_size)
    decay_copy.wait()
    tall = stacked(decay_ref[...])
    s_from = lax.broadcasted_iota(jnp.int32, (CHUNK, 2 * CHUNK), 0)
    s_to = lax.broadcasted_iota(jnp.int32, (CHUNK, 2 * CHUNK), 1)
    both = sums(tall, indicator((s_from > s_to) | (s_to >= CHUNK)))
    later = jnp.zeros((HEAD_ROWS, CHUNK), F32)
    for c in reversed(range(chunks)):
        part = both[c * HEAD_ROWS : (c + 1) * HEAD_ROWS]
        factor_ref[c] = pair_rows(jnp.exp(part[:, :CHUNK] + later))
        later = later + part[:, CHUNK:]
    gain = mm(pair_rows(jnp.exp(later[:, :HEAD_ROWS])), spread, TN)
    states = None
    for k in range(pieces):
        copies[2 * k].wait()
        copies[2 * k + 1].wait()
        where = pl.ds(k * rows, rows)
        here = range(k * rows // CHUNK, (k + 1) * rows // CHUNK)
        scaled = (signal_ref[where, :].astype(F32) * spread_rows(factor_ref, here, spread)).astype(BF16)
        term = mm(entry_ref[where, :], scaled, TN)
        states = term if states is None else states + term
    size = states.shape[0]
    if split:
        own_ref, first_ref, second_ref = outs
        half = width // 2
        for k in range(2):
            own_ref[k, :size, :] = states[:, k * half : (k + 1) * half]
            own_ref[k, size:, :] = gain[:, k * half : (k + 1) * half]

        @pl.when(place_ref[0] == 0)
        def _():
            first_ref[...] = own_ref[0]
            second_ref[...] = own_ref[1]

        @pl.when(place_ref[0] != 0)
        def _():
            first_ref[...] = own_ref[1]
            second_ref[...] = own_ref[0]
    else:
        (own_ref,) = outs
        own_ref[:size, :] = states
        own_ref[size:, :] = gain
    gate_copy.wait()


def local_states(place, decay, entry_map, signal, gate_input, head_size, split, pieces, parts):
    length, width = signal.shape
    state_size = entry_map.shape[1]
    tall = state_size + HEAD_ROWS
    if split:
        shapes = [(2, tall, width // 2), (tall, width // 2), (tall, width // 2)]
    else:
        shapes = [(tall, width)]
    return pl.pallas_call(
        functools.partial(state_kernel, split, head_size, pieces),
        in_specs=[pl.BlockSpec(memory_space=pltpu.SMEM)] + [IN_HBM] * 4,
        out_specs=[IN_VMEM] * (len(shapes) + 3),
        out_shape=[pltpu.VMEM(s, F32) for s in shapes]
        + [
            pltpu.VMEM((length, state_size), BF16),
            pltpu.VMEM((length, width), BF16),
            pltpu.VMEM((length // parts, width), BF16),
        ],
        scratch_shapes=[
            pltpu.VMEM((HEAD_ROWS, length), F32),
            pltpu.VMEM((length // CHUNK, 2 * HEAD_ROWS, CHUNK), BF16),
            pltpu.SemaphoreType.DMA((2 * pieces + 2,)),
        ],
        name="device_states",
        compiler_params=pltpu.CompilerParams(vmem_limit_bytes=52 << 20),
        cost_estimate=pl.CostEstimate(
            flops=2 * length * width * state_size,
            bytes_accessed=2 * length * (width + state_size),
            transcendentals=0,
        ),
    )(place, decay, entry_map, signal, gate_input)


def by_head(value, factor):
    rows, width = value.shape
    return (value.reshape(rows // HEAD_ROWS, HEAD_ROWS, width) * factor[None]).reshape(rows, width)


def local_kernel(base, head_size, group, decay_ref, readout_ref, gate_ref, entry_ref, signal_ref, state_in, *rest):
    inside_ref, share_ref, state_ref, in_ref, out_ref = rest
    length, width = signal_ref.shape
    sides, part_rows, side = inside_ref.shape
    first = base // CHUNK
    many = part_rows // CHUNK
    spread = spread_matrix(width, head_size)
    tall = stacked(decay_ref[...])
    half = CHUNK // 2
    s_from = lax.broadcasted_iota(jnp.int32, (CHUNK, CHUNK), 0)
    s_to = lax.broadcasted_iota(jnp.int32, (CHUNK, CHUNK), 1)
    early = (s_from < half).astype(F32)
    centred = ((s_from <= s_to).astype(F32) - early).astype(BF16)
    matrix = jnp.concatenate([centred, early.astype(BF16), (1.0 - early).astype(BF16)], axis=1)
    three = sums(tall, matrix)
    before = jnp.zeros((HEAD_ROWS, HEAD_ROWS), F32)
    to_here, to_next = [], []
    for c in range(first + many):
        part = three[c * HEAD_ROWS : (c + 1) * HEAD_ROWS]
        to_middle = part[:, CHUNK : CHUNK + HEAD_ROWS]
        onward = part[:, 2 * CHUNK : 2 * CHUNK + HEAD_ROWS]
        if c >= first:
            from_middle = part[:, :CHUNK]
            in_ref[c - first] = pair_rows(jnp.exp(-from_middle))
            out_ref[c - first] = pair_rows(jnp.exp(from_middle))
            to_here.append(pair_rows(jnp.exp(before + to_middle)))
            if (c + 1) * CHUNK < length:
                following = three[(c + 1) * HEAD_ROWS : (c + 2) * HEAD_ROWS, CHUNK : CHUNK + HEAD_ROWS]
                to_next.append(pair_rows(jnp.exp(onward + following)))
            else:
                to_next.append(pair_rows(jnp.exp(onward)))
        before = before + (to_middle + onward)
    causal = s_from >= s_to
    state = state_in[...] if base else jnp.zeros(state_ref.shape, F32)
    for start in range(0, many, group):
        here = range(start, start + group)
        where = pl.ds(base + start * CHUNK, group * CHUNK)
        there = pl.ds(start * CHUNK, group * CHUNK)
        cut = lambda value, j: value[j * CHUNK : (j + 1) * CHUNK]
        entry = entry_ref[where, :]
        readout = readout_ref[where, :]
        scaled = (signal_ref[where, :].astype(F32) * spread_rows(in_ref, here, spread)).astype(BF16)
        scores, added, passed = [], [], []
        for j in range(group):
            products = mm(cut(readout, j), cut(entry, j), NT)
            scores.append(jnp.where(causal, products, 0.0).astype(BF16))
            added.append(mm(cut(entry, j), cut(scaled, j), TN))
        for j in range(group):
            passed.append(state.astype(BF16))
            state = by_head(state + added[j], mm(to_next[start + j], spread, TN))
        output = jnp.concatenate(
            [
                mm(
                    jnp.concatenate([scores[j], cut(readout, j)], axis=1),
                    jnp.concatenate([cut(scaled, j), passed[j]], axis=0),
                )
                for j in range(group)
            ],
            axis=0,
        )
        gate = gate_ref[there if gate_ref.shape[0] == part_rows else where, :].astype(F32)
        opened = gate / (1.0 + jnp.exp(-gate)) * spread_rows(out_ref, here, spread)
        inside = (output * opened).astype(BF16)
        share = jnp.concatenate(
            [by_head(cut(opened, j), mm(to_here[start + j], spread, TN)) for j in range(group)], axis=0
        ).astype(BF16)
        for k in range(sides):
            inside_ref[k, there, :] = inside[:, k * side : (k + 1) * side]
            share_ref[k, there, :] = share[:, k * side : (k + 1) * side]
    state_ref[...] = state


def local_part(index, parts, decay, readout, gate_input, entry_map, signal, state, head_size, sides, group):
    length, width = signal.shape
    state_size = entry_map.shape[1]
    rows = length // parts
    return pl.pallas_call(
        functools.partial(local_kernel, index * rows, head_size, group),
        in_specs=[IN_VMEM] * 6,
        out_specs=[IN_VMEM] * 3,
        out_shape=[pltpu.VMEM((sides, rows, width // sides), BF16)] * 2 + [pltpu.VMEM((state_size, width), F32)],
        scratch_shapes=[pltpu.VMEM((rows // CHUNK, 2 * HEAD_ROWS, CHUNK), BF16)] * 2,
        name="local_part",
        compiler_params=pltpu.CompilerParams(vmem_limit_bytes=16 << 20),
        cost_estimate=pl.CostEstimate(
            flops=8 * length * width * state_size // parts,
            bytes_accessed=2 * length * (4 * width + 2 * state_size) // parts,
            transcendentals=length * width // parts,
        ),
    )(decay, readout, gate_input, entry_map, signal, state)


def final_kernel(turn, head_size, parts, rows, place_ref, *rest):
    count = 1 if turn is None else 2
    incoming, rest = rest[:count], rest[count:]
    readout_ref, gain_ref, *rest = rest
    groups, rest = [rest[2 * p : 2 * p + 2] for p in range(parts)], rest[2 * parts :]
    result_hbm, result_ref, terms_ref, semaphores = rest[-4:]
    size = readout_ref.shape[1]
    _, part_rows, width = groups[0][0].shape

    def keep(value):
        high, low = two_terms(value)
        terms_ref[:size, :] = high
        terms_ref[size:, :] = low

    if turn is None:
        side = 0
        keep(incoming[0][...])
    else:
        place = place_ref[0]
        side = jnp.where(place == 1, turn, 1 - turn)
        other = (place == 1) | (place == 2)

        @pl.when(other)
        def _():
            keep(incoming[0][...])

        @pl.when(jnp.logical_not(other))
        def _():
            keep(incoming[1][...])

    group = min(width, 256)
    row = lax.broadcasted_iota(jnp.int32, (group, group), 0)
    column = lax.broadcasted_iota(jnp.int32, (group, group), 1)
    same = lax.div(row, head_size) == lax.div(column, head_size)
    average = jnp.where(same, 1.0 / head_size, 0.0).astype(BF16)
    gain = gain_ref[side]
    terms = terms_ref[...]
    columns = pl.ds(0, width) if turn is None else pl.ds(pl.multiple_of(side * width, width), width)
    copies = []
    for p, (inside_ref, share_ref) in enumerate(groups):
        for start in range(0, part_rows, rows):
            where = pl.ds(start, rows)
            there = pl.ds(p * part_rows + start, rows)
            readout = readout_ref[there, :]
            across = mm(jnp.concatenate([readout, readout], axis=1), terms)
            gated = inside_ref[side, where, :].astype(F32) + share_ref[side, where, :].astype(F32) * across
            squares = (gated * gated).astype(BF16)
            mean = jnp.concatenate(
                [mm(squares[:, g : g + group], average) for g in range(0, width, group)], axis=1
            )
            result_ref[there, :] = (gated * lax.rsqrt(mean + EPSILON) * gain).astype(BF16)
            copy = pltpu.make_async_copy(
                result_ref.at[there], result_hbm.at[there, columns], semaphores.at[len(copies)]
            )
            copy.start()
            copies.append(copy)
    for copy in copies:
        copy.wait()


def final_part(turn, place, incoming, readout, norm_gain, groups, kept, head_size, rows):
    sides, part_rows, width = groups[0][0].shape
    length = part_rows * len(groups)
    state_size = readout.shape[1]
    arguments = [place, *incoming, readout, norm_gain, *[v for g in groups for v in g]]
    in_specs = [pl.BlockSpec(memory_space=pltpu.SMEM)] + [IN_VMEM] * (len(arguments) - 1)
    aliases = {}
    if kept is not None:
        aliases = {len(arguments): 0}
        arguments.append(kept)
        in_specs.append(IN_HBM)
    return pl.pallas_call(
        functools.partial(final_kernel, turn, head_size, len(groups), rows),
        in_specs=in_specs,
        out_specs=IN_HBM,
        out_shape=jax.ShapeDtypeStruct((length, width * sides), BF16),
        input_output_aliases=aliases,
        scratch_shapes=[
            pltpu.VMEM((length, width), BF16),
            pltpu.VMEM((2 * state_size, width), BF16),
            pltpu.SemaphoreType.DMA((length // rows,)),
        ],
        name="final_part",
        compiler_params=pltpu.CompilerParams(vmem_limit_bytes=16 << 20),
        cost_estimate=pl.CostEstimate(
            flops=4 * length * width * state_size,
            bytes_accessed=2 * length * (3 * width + state_size),
            transcendentals=length * width,
        ),
    )(*arguments)


def blend_kernel(place_ref, one_ref, two_ref, own_ref, first_ref, second_ref, kept_ref):
    size = kept_ref.shape[0]
    width = kept_ref.shape[1]

    def scaled(rows_ref, value):
        gain = rows_ref[size:, :]
        shape = (size // HEAD_ROWS, HEAD_ROWS, width)
        return (value.reshape(shape) * gain[None]).reshape(size, width)

    @pl.when(place_ref[0] == 1)
    def _():
        mine = own_ref.at[0]
        first = one_ref[:size, :]
        second = mine[:size, :] + scaled(mine, first)
        first_ref[...] = second
        second_ref[...] = two_ref[:size, :] + scaled(two_ref, second)
        kept_ref[...] = first

    @pl.when(place_ref[0] != 1)
    def _():
        mine = own_ref.at[1]
        first = two_ref[:size, :]
        second = one_ref[:size, :] + scaled(one_ref, first)
        second_ref[...] = second
        kept_ref[...] = second

        @pl.when(place_ref[0] == 0)
        def _():
            first_ref[...] = mine[:size, :]

        @pl.when(place_ref[0] != 0)
        def _():
            first_ref[...] = mine[:size, :] + scaled(mine, second)


def blend(place, one, two, own):
    size = one.shape[0] - HEAD_ROWS
    width = one.shape[1]
    return pl.pallas_call(
        blend_kernel,
        in_specs=[pl.BlockSpec(memory_space=pltpu.SMEM)] + [IN_VMEM] * 3,
        out_specs=[IN_VMEM] * 3,
        out_shape=[pltpu.VMEM((size, width), F32)] * 3,
        name="blend",
        compiler_params=pltpu.CompilerParams(vmem_limit_bytes=4 << 20),
    )(place, one, two, own)


def scan_devices(own, devices):
    size = own.shape[0] - HEAD_ROWS
    gain = lambda v: v[size : size + 1]
    reach, before = own, None
    shift = 1
    while shift < devices:
        came = lax.ppermute(reach, "tm", [(i, i + shift) for i in range(devices - shift)])
        join = lambda later: jnp.concatenate(
            [later[:size] + gain(later) * came[:size], later[size:] * came[size:]], axis=0
        )
        before = came if before is None else join(before)
        reach = join(reach)
        shift *= 2
    if before is None:
        return jnp.zeros_like(own[:size])
    return before[:size]


def shards(devices, signal, entry_map, readout, gate_input, log_decay, norm_gain):
    heads, length = log_decay.shape
    width = signal.shape[1]
    head_size = width // heads
    split = devices == 4 and width % 256 == 0
    sides = 2 if split else 1
    decay = log_decay
    if heads < HEAD_ROWS:
        decay = jnp.pad(log_decay, ((0, HEAD_ROWS - heads), (0, 0)))
    place = lax.axis_index("tm").astype(jnp.int32).reshape(1)
    *made, entry_map, signal, gate_first = local_states(
        place, decay, entry_map, signal, gate_input, head_size, split, 4, 2
    )
    common = (entry_map, signal)
    nothing = jnp.zeros((8, 128), F32)
    if split:
        own, first, second = made
        one = lax.ppermute(first, "tm", [(0, 1), (1, 2)])
        two = lax.ppermute(second, "tm", [(2, 1), (0, 2)])
    *before, state = local_part(0, 2, decay, readout, gate_first, *common, nothing, head_size, sides, 4)
    if split:
        one, two, state = lax.optimization_barrier((one, two, state))
        first, second, kept = blend(place, one, two, own)
        one = lax.ppermute(first, "tm", [(0, 1), (1, 2), (2, 3)])
        two = lax.ppermute(second, "tm", [(1, 3)])
    else:
        total = scan_devices(made[0], devices)
    *after, _ = local_part(1, 2, decay, readout, gate_input, *common, state, head_size, sides, 4)
    common = (readout, norm_gain.reshape(sides, 1, width // sides), (before, after))
    if split:
        result = final_part(0, place, (kept, one), *common, None, head_size, 1024)
        return final_part(1, place, (one, two), *common, result, head_size, 1024)
    return final_part(None, place, (total,), *common, None, head_size, 1024)


def solution(mesh):
    in_specs = (
        P(("parts", "tm"), ("head", "sub")),
        P(("parts", "tm"), None),
        P(("parts", "tm"), None),
        P(("parts", "tm"), ("head", "sub")),
        P(("head", "sub"), ("parts", "tm")),
        P(("head", "sub")),
    )
    out_specs = P(("parts", "tm"), ("head", "sub"))
    body = functools.partial(shards, mesh.shape["tm"])
    return jax.shard_map(body, mesh=mesh, in_specs=in_specs, out_specs=out_specs, check_vma=False)
```

```python
import functools

import jax
import jax.numpy as jnp
from jax import lax
from jax.experimental import pallas as pl
from jax.experimental.pallas import tpu as pltpu
from jax.sharding import PartitionSpec as P

CHUNK = 128
HEAD_ROWS = 8
EPSILON = 1e-05
F32 = jnp.float32
BF16 = jnp.bfloat16
TN = (((0,), (0,)), ((), ()))
NT = (((1,), (1,)), ((), ()))
IN_HBM = pl.BlockSpec(memory_space=pltpu.HBM)
IN_VMEM = pl.BlockSpec(memory_space=pltpu.VMEM)


def mm(left, right, dims=(((1,), (0,)), ((), ()))):
    return lax.dot_general(left, right, dims, preferred_element_type=F32)


def two_terms(value):
    high = value.astype(BF16)
    return high, (value - high.astype(F32)).astype(BF16)


def spread_matrix(width, head_size):
    row = lax.broadcasted_iota(jnp.int32, (2 * HEAD_ROWS, width), 0)
    column = lax.broadcasted_iota(jnp.int32, (2 * HEAD_ROWS, width), 1)
    own = lax.rem(row, HEAD_ROWS) == lax.div(column, head_size)
    return own.astype(F32).astype(BF16)


def stacked(decay):
    chunks = decay.shape[1] // CHUNK
    return jnp.concatenate([decay[:, c * CHUNK : (c + 1) * CHUNK] for c in range(chunks)], axis=0)


def sums(decay_rows, matrix):
    high = decay_rows.astype(BF16)
    rest = decay_rows - high.astype(F32)
    middle = rest.astype(BF16)
    low = (rest - middle.astype(F32)).astype(BF16)
    return mm(high, matrix) + (mm(middle, matrix) + mm(low, matrix))


def pair_rows(value):
    high, low = two_terms(value)
    return jnp.concatenate([high, low], axis=0)


def indicator(test):
    return test.astype(F32).astype(BF16)


def spread_rows(factor_ref, chunks, spread):
    return jnp.concatenate([mm(factor_ref[c], spread, TN) for c in chunks], axis=0)


def copy_rows(source, target, semaphore, start, rows):
    where = pl.ds(start, rows)
    return pltpu.make_async_copy(source.at[where], target.at[where], semaphore)


def state_kernel(split, head_size, pieces, place_ref, decay_hbm, entry_hbm, signal_hbm, gate_hbm, *rest):
    outs, (entry_ref, signal_ref, gate_ref, decay_ref, factor_ref, semaphores) = rest[:-6], rest[-6:]
    length, width = signal_ref.shape
    rows = length // pieces
    chunks = length // CHUNK
    decay_copy = pltpu.make_async_copy(decay_hbm, decay_ref, semaphores.at[2 * pieces])
    decay_copy.start()
    copies = []
    for k in range(pieces):
        copies.append(copy_rows(entry_hbm, entry_ref, semaphores.at[k], k * rows, rows))
        copies.append(copy_rows(signal_hbm, signal_ref, semaphores.at[pieces + k], k * rows, rows))
    for copy in copies:
        copy.start()
    gate_copy = pltpu.make_async_copy(
        gate_hbm.at[pl.ds(0, gate_ref.shape[0])], gate_ref, semaphores.at[2 * pieces + 1]
    )
    gate_copy.start()
    spread = spread_matrix(width, head_size)
    decay_copy.wait()
    tall = stacked(decay_ref[...])
    s_from = lax.broadcasted_iota(jnp.int32, (CHUNK, 2 * CHUNK), 0)
    s_to = lax.broadcasted_iota(jnp.int32, (CHUNK, 2 * CHUNK), 1)
    both = sums(tall, indicator((s_from > s_to) | (s_to >= CHUNK)))
    later = jnp.zeros((HEAD_ROWS, CHUNK), F32)
    for c in reversed(range(chunks)):
        part = both[c * HEAD_ROWS : (c + 1) * HEAD_ROWS]
        factor_ref[c] = pair_rows(jnp.exp(part[:, :CHUNK] + later))
        later = later + part[:, CHUNK:]
    gain = mm(pair_rows(jnp.exp(later[:, :HEAD_ROWS])), spread, TN)
    states = None
    for k in range(pieces):
        copies[2 * k].wait()
        copies[2 * k + 1].wait()
        where = pl.ds(k * rows, rows)
        here = range(k * rows // CHUNK, (k + 1) * rows // CHUNK)
        scaled = (signal_ref[where, :].astype(F32) * spread_rows(factor_ref, here, spread)).astype(BF16)
        term = mm(entry_ref[where, :], scaled, TN)
        states = term if states is None else states + term
    size = states.shape[0]
    if split:
        own_ref, first_ref, second_ref = outs
        half = width // 2
        for k in range(2):
            own_ref[k, :size, :] = states[:, k * half : (k + 1) * half]
            own_ref[k, size:, :] = gain[:, k * half : (k + 1) * half]

        @pl.when(place_ref[0] == 0)
        def _():
            first_ref[...] = own_ref[0]
            second_ref[...] = own_ref[1]

        @pl.when(place_ref[0] != 0)
        def _():
            first_ref[...] = own_ref[1]
            second_ref[...] = own_ref[0]
    else:
        (own_ref,) = outs
        own_ref[:size, :] = states
        own_ref[size:, :] = gain
    gate_copy.wait()


def local_states(place, decay, entry_map, signal, gate_input, head_size, split, pieces, gate_rows):
    length, width = signal.shape
    state_size = entry_map.shape[1]
    tall = state_size + HEAD_ROWS
    if split:
        shapes = [(2, tall, width // 2), (tall, width // 2), (tall, width // 2)]
    else:
        shapes = [(tall, width)]
    return pl.pallas_call(
        functools.partial(state_kernel, split, head_size, pieces),
        in_specs=[pl.BlockSpec(memory_space=pltpu.SMEM)] + [IN_HBM] * 4,
        out_specs=[IN_VMEM] * (len(shapes) + 3),
        out_shape=[pltpu.VMEM(s, F32) for s in shapes]
        + [
            pltpu.VMEM((length, state_size), BF16),
            pltpu.VMEM((length, width), BF16),
            pltpu.VMEM((gate_rows, width), BF16),
        ],
        scratch_shapes=[
            pltpu.VMEM((HEAD_ROWS, length), F32),
            pltpu.VMEM((length // CHUNK, 2 * HEAD_ROWS, CHUNK), BF16),
            pltpu.SemaphoreType.DMA((2 * pieces + 2,)),
        ],
        name="device_states",
        compiler_params=pltpu.CompilerParams(vmem_limit_bytes=52 << 20),
        cost_estimate=pl.CostEstimate(
            flops=2 * length * width * state_size,
            bytes_accessed=2 * length * (width + state_size),
            transcendentals=0,
        ),
    )(place, decay, entry_map, signal, gate_input)


def by_head(value, factor):
    rows, width = value.shape
    return (value.reshape(rows // HEAD_ROWS, HEAD_ROWS, width) * factor[None]).reshape(rows, width)


def local_kernel(base, head_size, group, decay_ref, readout_ref, gate_ref, entry_ref, signal_ref, state_in, *rest):
    inside_ref, share_ref, state_ref, in_ref, out_ref = rest
    length, width = signal_ref.shape
    part_rows = inside_ref.shape[0]
    first = base // CHUNK
    many = part_rows // CHUNK
    spread = spread_matrix(width, head_size)
    tall = stacked(decay_ref[...])
    half = CHUNK // 2
    s_from = lax.broadcasted_iota(jnp.int32, (CHUNK, CHUNK), 0)
    s_to = lax.broadcasted_iota(jnp.int32, (CHUNK, CHUNK), 1)
    early = (s_from < half).astype(F32)
    centred = ((s_from <= s_to).astype(F32) - early).astype(BF16)
    matrix = jnp.concatenate([centred, early.astype(BF16), (1.0 - early).astype(BF16)], axis=1)
    three = sums(tall, matrix)
    before = jnp.zeros((HEAD_ROWS, HEAD_ROWS), F32)
    to_here, to_next = [], []
    for c in range(first + many):
        part = three[c * HEAD_ROWS : (c + 1) * HEAD_ROWS]
        to_middle = part[:, CHUNK : CHUNK + HEAD_ROWS]
        onward = part[:, 2 * CHUNK : 2 * CHUNK + HEAD_ROWS]
        if c >= first:
            from_middle = part[:, :CHUNK]
            frames = slice((c - first) * CHUNK, (c - first + 1) * CHUNK)
            in_ref[:, frames] = pair_rows(jnp.exp(-from_middle))
            out_ref[:, frames] = pair_rows(jnp.exp(from_middle))
            to_here.append(pair_rows(jnp.exp(before + to_middle)))
            if (c + 1) * CHUNK < length:
                following = three[(c + 1) * HEAD_ROWS : (c + 2) * HEAD_ROWS, CHUNK : CHUNK + HEAD_ROWS]
                to_next.append(pair_rows(jnp.exp(onward + following)))
            else:
                to_next.append(pair_rows(jnp.exp(onward)))
        before = before + (to_middle + onward)
    causal = s_from >= s_to
    state = state_in[...] if base else jnp.zeros(state_ref.shape, F32)
    for start in range(0, many, group):
        count = min(group, many - start)
        where = pl.ds(base + start * CHUNK, count * CHUNK)
        there = pl.ds(start * CHUNK, count * CHUNK)
        cut = lambda value, j: value[j * CHUNK : (j + 1) * CHUNK]
        entry = entry_ref[where, :]
        readout = readout_ref[where, :]
        scaled = (signal_ref[where, :].astype(F32) * mm(in_ref[:, there], spread, TN)).astype(BF16)
        scores, added, passed = [], [], []
        for j in range(count):
            products = mm(cut(readout, j), cut(entry, j), NT)
            scores.append(jnp.where(causal, products, 0.0).astype(BF16))
            added.append(mm(cut(entry, j), cut(scaled, j), TN))
        for j in range(count):
            passed.append(state.astype(BF16))
            state = by_head(state + added[j], mm(to_next[start + j], spread, TN))
        output = jnp.concatenate(
            [
                mm(
                    jnp.concatenate([scores[j], cut(readout, j)], axis=1),
                    jnp.concatenate([cut(scaled, j), passed[j]], axis=0),
                )
                for j in range(count)
            ],
            axis=0,
        )
        gate = gate_ref[there if gate_ref.shape[0] == part_rows else where, :].astype(F32)
        opened = gate / (1.0 + jnp.exp(-gate)) * mm(out_ref[:, there], spread, TN)
        inside_ref[there, :] = (output * opened).astype(BF16)
        share_ref[there, :] = jnp.concatenate(
            [by_head(cut(opened, j), mm(to_here[start + j], spread, TN)) for j in range(count)], axis=0
        ).astype(BF16)
    state_ref[...] = state


def local_part(base, rows, decay, readout, gate_input, entry_map, signal, state, head_size, group):
    length, width = signal.shape
    state_size = entry_map.shape[1]
    return pl.pallas_call(
        functools.partial(local_kernel, base, head_size, group),
        in_specs=[IN_VMEM] * 6,
        out_specs=[IN_VMEM] * 3,
        out_shape=[pltpu.VMEM((rows, width), BF16)] * 2 + [pltpu.VMEM((state_size, width), F32)],
        scratch_shapes=[pltpu.VMEM((2 * HEAD_ROWS, rows), BF16)] * 2,
        name="local_part",
        compiler_params=pltpu.CompilerParams(vmem_limit_bytes=16 << 20),
        cost_estimate=pl.CostEstimate(
            flops=8 * rows * width * state_size,
            bytes_accessed=2 * rows * (4 * width + 2 * state_size),
            transcendentals=rows * width,
        ),
    )(decay, readout, gate_input, entry_map, signal, state)


def final_kernel(count, head_size, parts, rows, place_ref, *rest):
    incoming, rest = rest[:count], rest[count:]
    readout_ref, gain_ref, *rest = rest
    groups, rest = [rest[2 * p : 2 * p + 2] for p in range(parts)], rest[2 * parts :]
    result_hbm, result_ref, terms_ref, semaphores = rest
    size = readout_ref.shape[1]
    width = gain_ref.shape[1]

    def keep(value_ref, at):
        high, low = two_terms(value_ref[...])
        terms_ref[:size, at : at + value_ref.shape[1]] = high
        terms_ref[size:, at : at + value_ref.shape[1]] = low

    if count == 1:
        keep(incoming[0], 0)
    else:
        one, two, kept = incoming
        place = place_ref[0]
        half = width // 2

        @pl.when(place == 1)
        def _():
            keep(kept, 0)
            keep(one, half)

        @pl.when(place == 2)
        def _():
            keep(one, 0)
            keep(kept, half)

        @pl.when((place != 1) & (place != 2))
        def _():
            keep(two, 0)
            keep(one, half)

    group = min(width, 256)
    row = lax.broadcasted_iota(jnp.int32, (group, group), 0)
    column = lax.broadcasted_iota(jnp.int32, (group, group), 1)
    same = lax.div(row, head_size) == lax.div(column, head_size)
    average = jnp.where(same, 1.0 / head_size, 0.0).astype(BF16)
    gain = gain_ref[...]
    terms = terms_ref[...]
    copies = []
    first = 0
    for inside_ref, share_ref in groups:
        for start in range(0, inside_ref.shape[0], rows):
            many = min(rows, inside_ref.shape[0] - start)
            where = pl.ds(start, many)
            there = pl.ds(first + start, many)
            readout = readout_ref[there, :]
            across = mm(jnp.concatenate([readout, readout], axis=1), terms)
            gated = inside_ref[where, :].astype(F32) + share_ref[where, :].astype(F32) * across
            squares = gated.astype(BF16) * gated.astype(BF16)
            mean = jnp.concatenate(
                [mm(squares[:, g : g + group], average) for g in range(0, width, group)], axis=1
            )
            result_ref[there, :] = (gated * lax.rsqrt(mean + EPSILON) * gain).astype(BF16)
            copy = pltpu.make_async_copy(result_ref.at[there], result_hbm.at[there], semaphores.at[len(copies)])
            copy.start()
            copies.append(copy)
        first += inside_ref.shape[0]
    for copy in copies:
        copy.wait()


def final_part(place, incoming, readout, norm_gain, groups, head_size, rows):
    length, state_size = readout.shape
    width = norm_gain.shape[1]
    arguments = [place, *incoming, readout, norm_gain, *[v for g in groups for v in g]]
    return pl.pallas_call(
        functools.partial(final_kernel, len(incoming), head_size, len(groups), rows),
        in_specs=[pl.BlockSpec(memory_space=pltpu.SMEM)] + [IN_VMEM] * (len(arguments) - 1),
        out_specs=IN_HBM,
        out_shape=jax.ShapeDtypeStruct((length, width), BF16),
        scratch_shapes=[
            pltpu.VMEM((length, width), BF16),
            pltpu.VMEM((2 * state_size, width), BF16),
            pltpu.SemaphoreType.DMA((length // rows + len(groups),)),
        ],
        name="final_part",
        compiler_params=pltpu.CompilerParams(vmem_limit_bytes=16 << 20),
        cost_estimate=pl.CostEstimate(
            flops=4 * length * width * state_size,
            bytes_accessed=2 * length * (3 * width + state_size),
            transcendentals=length * width,
        ),
    )(*arguments)


def blend_kernel(place_ref, one_ref, two_ref, own_ref, first_ref, second_ref, kept_ref):
    size = kept_ref.shape[0]
    width = kept_ref.shape[1]

    def scaled(rows_ref, value):
        gain = rows_ref[size:, :]
        shape = (size // HEAD_ROWS, HEAD_ROWS, width)
        return (value.reshape(shape) * gain[None]).reshape(size, width)

    @pl.when(place_ref[0] == 1)
    def _():
        mine = own_ref.at[0]
        first = one_ref[:size, :]
        second = mine[:size, :] + scaled(mine, first)
        first_ref[...] = second
        second_ref[...] = two_ref[:size, :] + scaled(two_ref, second)
        kept_ref[...] = first

    @pl.when(place_ref[0] != 1)
    def _():
        mine = own_ref.at[1]
        first = two_ref[:size, :]
        second = one_ref[:size, :] + scaled(one_ref, first)
        second_ref[...] = second
        kept_ref[...] = second

        @pl.when(place_ref[0] == 0)
        def _():
            first_ref[...] = mine[:size, :]

        @pl.when(place_ref[0] != 0)
        def _():
            first_ref[...] = mine[:size, :] + scaled(mine, second)


def blend(place, one, two, own):
    size = one.shape[0] - HEAD_ROWS
    width = one.shape[1]
    return pl.pallas_call(
        blend_kernel,
        in_specs=[pl.BlockSpec(memory_space=pltpu.SMEM)] + [IN_VMEM] * 3,
        out_specs=[IN_VMEM] * 3,
        out_shape=[pltpu.VMEM((size, width), F32)] * 3,
        name="blend",
        compiler_params=pltpu.CompilerParams(vmem_limit_bytes=4 << 20),
    )(place, one, two, own)


def scan_devices(own, devices):
    size = own.shape[0] - HEAD_ROWS
    gain = lambda v: v[size : size + 1]
    reach, before = own, None
    shift = 1
    while shift < devices:
        came = lax.ppermute(reach, "tm", [(i, i + shift) for i in range(devices - shift)])
        join = lambda later: jnp.concatenate(
            [later[:size] + gain(later) * came[:size], later[size:] * came[size:]], axis=0
        )
        before = came if before is None else join(before)
        reach = join(reach)
        shift *= 2
    if before is None:
        return jnp.zeros_like(own[:size])
    return before[:size]


def shards(devices, signal, entry_map, readout, gate_input, log_decay, norm_gain):
    heads, length = log_decay.shape
    width = signal.shape[1]
    head_size = width // heads
    split = devices == 4 and width % 256 == 0
    early = length * 10 // 16
    late = length - early
    decay = log_decay
    if heads < HEAD_ROWS:
        decay = jnp.pad(log_decay, ((0, HEAD_ROWS - heads), (0, 0)))
    place = lax.axis_index("tm").astype(jnp.int32).reshape(1)
    *made, entry_map, signal, gate_first = local_states(
        place, decay, entry_map, signal, gate_input, head_size, split, 4, early
    )
    common = (entry_map, signal)
    nothing = jnp.zeros((8, 128), F32)
    if split:
        own, first, second = made
        one = lax.ppermute(first, "tm", [(0, 1), (1, 2)])
        two = lax.ppermute(second, "tm", [(2, 1), (0, 2)])
    *before, state = local_part(0, early, decay, readout, gate_first, *common, nothing, head_size, 8)
    if split:
        one, two, state = lax.optimization_barrier((one, two, state))
        first, second, kept = blend(place, one, two, own)
        one = lax.ppermute(first, "tm", [(0, 1), (1, 2), (2, 3)])
        two = lax.ppermute(second, "tm", [(1, 3)])
        incoming = (one, two, kept)
    else:
        incoming = (scan_devices(made[0], devices),)
    *after, _ = local_part(early, late, decay, readout, gate_input, *common, state, head_size, 8)
    gain = norm_gain.reshape(1, width)
    return final_part(place, incoming, readout, gain, (before, after), head_size, 512)


def solution(mesh):
    in_specs = (
        P(("parts", "tm"), ("head", "sub")),
        P(("parts", "tm"), None),
        P(("parts", "tm"), None),
        P(("parts", "tm"), ("head", "sub")),
        P(("head", "sub"), ("parts", "tm")),
        P(("head", "sub")),
    )
    out_specs = P(("parts", "tm"), ("head", "sub"))
    body = functools.partial(shards, mesh.shape["tm"])
    return jax.shard_map(body, mesh=mesh, in_specs=in_specs, out_specs=out_specs, check_vma=False)
```

```python
import functools

import jax
import jax.numpy as jnp
from jax import lax
from jax.experimental import pallas as pl
from jax.experimental.pallas import tpu as pltpu
from jax.sharding import PartitionSpec as P

CHUNK = 128
HEAD_ROWS = 8
EPSILON = 1e-05
F32 = jnp.float32
BF16 = jnp.bfloat16
TN = (((0,), (0,)), ((), ()))
NT = (((1,), (1,)), ((), ()))
IN_HBM = pl.BlockSpec(memory_space=pltpu.HBM)
IN_VMEM = pl.BlockSpec(memory_space=pltpu.VMEM)


def mm(left, right, dims=(((1,), (0,)), ((), ()))):
    return lax.dot_general(left, right, dims, preferred_element_type=F32)


def two_terms(value):
    high = value.astype(BF16)
    return high, (value - high.astype(F32)).astype(BF16)


def spread_matrix(width, head_size):
    row = lax.broadcasted_iota(jnp.int32, (2 * HEAD_ROWS, width), 0)
    column = lax.broadcasted_iota(jnp.int32, (2 * HEAD_ROWS, width), 1)
    own = lax.rem(row, HEAD_ROWS) == lax.div(column, head_size)
    return own.astype(F32).astype(BF16)


def stacked(decay):
    chunks = decay.shape[1] // CHUNK
    return jnp.concatenate([decay[:, c * CHUNK : (c + 1) * CHUNK] for c in range(chunks)], axis=0)


def sums(decay_rows, matrix):
    high = decay_rows.astype(BF16)
    rest = decay_rows - high.astype(F32)
    middle = rest.astype(BF16)
    low = (rest - middle.astype(F32)).astype(BF16)
    return mm(high, matrix) + (mm(middle, matrix) + mm(low, matrix))


def pair_rows(value):
    high, low = two_terms(value)
    return jnp.concatenate([high, low], axis=0)


def indicator(test):
    return test.astype(F32).astype(BF16)


def spread_rows(factor_ref, chunks, spread):
    return jnp.concatenate([mm(factor_ref[c], spread, TN) for c in chunks], axis=0)


def copy_rows(source, target, semaphore, start, rows):
    where = pl.ds(start, rows)
    return pltpu.make_async_copy(source.at[where], target.at[where], semaphore)


def state_kernel(split, head_size, pieces, place_ref, decay_hbm, entry_hbm, signal_hbm, gate_hbm, *rest):
    outs, (entry_ref, signal_ref, gate_ref, decay_ref, factor_ref, semaphores) = rest[:-6], rest[-6:]
    length, width = signal_ref.shape
    rows = length // pieces
    chunks = length // CHUNK
    decay_copy = pltpu.make_async_copy(decay_hbm, decay_ref, semaphores.at[2 * pieces])
    decay_copy.start()
    copies = []
    for k in range(pieces):
        copies.append(copy_rows(entry_hbm, entry_ref, semaphores.at[k], k * rows, rows))
        copies.append(copy_rows(signal_hbm, signal_ref, semaphores.at[pieces + k], k * rows, rows))
    for copy in copies:
        copy.start()
    gate_copy = pltpu.make_async_copy(
        gate_hbm.at[pl.ds(0, gate_ref.shape[0])], gate_ref, semaphores.at[2 * pieces + 1]
    )
    gate_copy.start()
    spread = spread_matrix(width, head_size)
    decay_copy.wait()
    tall = stacked(decay_ref[...])
    s_from = lax.broadcasted_iota(jnp.int32, (CHUNK, 2 * CHUNK), 0)
    s_to = lax.broadcasted_iota(jnp.int32, (CHUNK, 2 * CHUNK), 1)
    both = sums(tall, indicator((s_from > s_to) | (s_to >= CHUNK)))
    later = jnp.zeros((HEAD_ROWS, CHUNK), F32)
    for c in reversed(range(chunks)):
        part = both[c * HEAD_ROWS : (c + 1) * HEAD_ROWS]
        factor_ref[c] = pair_rows(jnp.exp(part[:, :CHUNK] + later))
        later = later + part[:, CHUNK:]
    gain = mm(pair_rows(jnp.exp(later[:, :HEAD_ROWS])), spread, TN)
    states = None
    for k in range(pieces):
        copies[2 * k].wait()
        copies[2 * k + 1].wait()
        where = pl.ds(k * rows, rows)
        here = range(k * rows // CHUNK, (k + 1) * rows // CHUNK)
        scaled = (signal_ref[where, :].astype(F32) * spread_rows(factor_ref, here, spread)).astype(BF16)
        term = mm(entry_ref[where, :], scaled, TN)
        states = term if states is None else states + term
    size = states.shape[0]
    if split:
        own_ref, first_ref, second_ref = outs
        half = width // 2
        for k in range(2):
            own_ref[k, :size, :] = states[:, k * half : (k + 1) * half]
            own_ref[k, size:, :] = gain[:, k * half : (k + 1) * half]

        @pl.when(place_ref[0] == 0)
        def _():
            first_ref[...] = own_ref[0]
            second_ref[...] = own_ref[1]

        @pl.when(place_ref[0] != 0)
        def _():
            first_ref[...] = own_ref[1]
            second_ref[...] = own_ref[0]
    else:
        (own_ref,) = outs
        own_ref[:size, :] = states
        own_ref[size:, :] = gain
    gate_copy.wait()


def local_states(place, decay, entry_map, signal, gate_input, head_size, split, pieces, gate_rows):
    length, width = signal.shape
    state_size = entry_map.shape[1]
    tall = state_size + HEAD_ROWS
    if split:
        shapes = [(2, tall, width // 2), (tall, width // 2), (tall, width // 2)]
    else:
        shapes = [(tall, width)]
    return pl.pallas_call(
        functools.partial(state_kernel, split, head_size, pieces),
        in_specs=[pl.BlockSpec(memory_space=pltpu.SMEM)] + [IN_HBM] * 4,
        out_specs=[IN_VMEM] * (len(shapes) + 3),
        out_shape=[pltpu.VMEM(s, F32) for s in shapes]
        + [
            pltpu.VMEM((length, state_size), BF16),
            pltpu.VMEM((length, width), BF16),
            pltpu.VMEM((gate_rows, width), BF16),
        ],
        scratch_shapes=[
            pltpu.VMEM((HEAD_ROWS, length), F32),
            pltpu.VMEM((length // CHUNK, 2 * HEAD_ROWS, CHUNK), BF16),
            pltpu.SemaphoreType.DMA((2 * pieces + 2,)),
        ],
        name="device_states",
        compiler_params=pltpu.CompilerParams(vmem_limit_bytes=52 << 20),
        cost_estimate=pl.CostEstimate(
            flops=2 * length * width * state_size,
            bytes_accessed=2 * length * (width + state_size),
            transcendentals=0,
        ),
    )(place, decay, entry_map, signal, gate_input)


def by_head(value, factor):
    rows, width = value.shape
    return (value.reshape(rows // HEAD_ROWS, HEAD_ROWS, width) * factor[None]).reshape(rows, width)


def local_kernel(base, head_size, group, decay_ref, readout_ref, gate_ref, entry_ref, signal_ref, state_in, *rest):
    inside_ref, share_ref, state_ref, in_ref, out_ref = rest
    length, width = signal_ref.shape
    part_rows = inside_ref.shape[0]
    first = base // CHUNK
    many = part_rows // CHUNK
    spread = spread_matrix(width, head_size)
    tall = stacked(decay_ref[...])
    half = CHUNK // 2
    s_from = lax.broadcasted_iota(jnp.int32, (CHUNK, CHUNK), 0)
    s_to = lax.broadcasted_iota(jnp.int32, (CHUNK, CHUNK), 1)
    early = (s_from < half).astype(F32)
    centred = ((s_from <= s_to).astype(F32) - early).astype(BF16)
    matrix = jnp.concatenate([centred, early.astype(BF16), (1.0 - early).astype(BF16)], axis=1)
    three = sums(tall, matrix)
    before = jnp.zeros((HEAD_ROWS, HEAD_ROWS), F32)
    to_here, to_next = [], []
    for c in range(first + many):
        part = three[c * HEAD_ROWS : (c + 1) * HEAD_ROWS]
        to_middle = part[:, CHUNK : CHUNK + HEAD_ROWS]
        onward = part[:, 2 * CHUNK : 2 * CHUNK + HEAD_ROWS]
        if c >= first:
            from_middle = part[:, :CHUNK]
            frames = slice((c - first) * CHUNK, (c - first + 1) * CHUNK)
            in_ref[:, frames] = pair_rows(jnp.exp(-from_middle))
            out_ref[:, frames] = pair_rows(jnp.exp(from_middle))
            to_here.append(pair_rows(jnp.exp(before + to_middle)))
            if (c + 1) * CHUNK < length:
                following = three[(c + 1) * HEAD_ROWS : (c + 2) * HEAD_ROWS, CHUNK : CHUNK + HEAD_ROWS]
                to_next.append(pair_rows(jnp.exp(onward + following)))
            else:
                to_next.append(pair_rows(jnp.exp(onward)))
        before = before + (to_middle + onward)
    causal = s_from >= s_to
    state = state_in[...] if base else jnp.zeros(state_ref.shape, F32)
    for start in range(0, many, group):
        count = min(group, many - start)
        where = pl.ds(base + start * CHUNK, count * CHUNK)
        there = pl.ds(start * CHUNK, count * CHUNK)
        cut = lambda value, j: value[j * CHUNK : (j + 1) * CHUNK]
        entry = entry_ref[where, :]
        readout = readout_ref[where, :]
        scaled = (signal_ref[where, :].astype(F32) * mm(in_ref[:, there], spread, TN)).astype(BF16)
        scores, added, passed = [], [], []
        for j in range(count):
            products = mm(cut(readout, j), cut(entry, j), NT)
            scores.append(jnp.where(causal, products, 0.0).astype(BF16))
            added.append(mm(cut(entry, j), cut(scaled, j), TN))
        for j in range(count):
            passed.append(state.astype(BF16))
            state = by_head(state + added[j], mm(to_next[start + j], spread, TN))
        output = jnp.concatenate(
            [
                mm(
                    jnp.concatenate([scores[j], cut(readout, j)], axis=1),
                    jnp.concatenate([cut(scaled, j), passed[j]], axis=0),
                )
                for j in range(count)
            ],
            axis=0,
        )
        gate = gate_ref[there if gate_ref.shape[0] == part_rows else where, :].astype(F32)
        opened = gate / (1.0 + jnp.exp(-gate)) * mm(out_ref[:, there], spread, TN)
        inside_ref[there, :] = (output * opened).astype(BF16)
        share_ref[there, :] = jnp.concatenate(
            [by_head(cut(opened, j), mm(to_here[start + j], spread, TN)) for j in range(count)], axis=0
        ).astype(BF16)
    state_ref[...] = state


def local_part(base, rows, decay, readout, gate_input, entry_map, signal, state, head_size, group):
    length, width = signal.shape
    state_size = entry_map.shape[1]
    return pl.pallas_call(
        functools.partial(local_kernel, base, head_size, group),
        in_specs=[IN_VMEM] * 6,
        out_specs=[IN_VMEM] * 3,
        out_shape=[pltpu.VMEM((rows, width), BF16)] * 2 + [pltpu.VMEM((state_size, width), F32)],
        scratch_shapes=[pltpu.VMEM((2 * HEAD_ROWS, rows), BF16)] * 2,
        name="local_part",
        compiler_params=pltpu.CompilerParams(vmem_limit_bytes=16 << 20),
        cost_estimate=pl.CostEstimate(
            flops=8 * rows * width * state_size,
            bytes_accessed=2 * rows * (4 * width + 2 * state_size),
            transcendentals=rows * width,
        ),
    )(decay, readout, gate_input, entry_map, signal, state)


def final_kernel(count, head_size, parts, cuts, place_ref, *rest):
    incoming, rest = rest[:count], rest[count:]
    readout_ref, gain_ref, *rest = rest
    groups, rest = [rest[2 * p : 2 * p + 2] for p in range(parts)], rest[2 * parts :]
    result_hbm, result_ref, terms_ref, semaphores = rest
    size = readout_ref.shape[1]
    width = gain_ref.shape[1]

    def keep(value_ref, at):
        high, low = two_terms(value_ref[...])
        terms_ref[:size, at : at + value_ref.shape[1]] = high
        terms_ref[size:, at : at + value_ref.shape[1]] = low

    if count == 1:
        keep(incoming[0], 0)
    else:
        one, two, kept = incoming
        place = place_ref[0]
        half = width // 2

        @pl.when(place == 1)
        def _():
            keep(kept, 0)
            keep(one, half)

        @pl.when(place == 2)
        def _():
            keep(one, 0)
            keep(kept, half)

        @pl.when((place != 1) & (place != 2))
        def _():
            keep(two, 0)
            keep(one, half)

    group = min(width, 256)
    row = lax.broadcasted_iota(jnp.int32, (group, group), 0)
    column = lax.broadcasted_iota(jnp.int32, (group, group), 1)
    same = lax.div(row, head_size) == lax.div(column, head_size)
    average = jnp.where(same, 1.0 / head_size, 0.0).astype(BF16)
    gain = gain_ref[...]
    terms = terms_ref[...]
    copies = []
    first = 0
    for inside_ref, share_ref in groups:
        rows = inside_ref.shape[0] // cuts
        for start in range(0, inside_ref.shape[0], rows):
            where = pl.ds(start, rows)
            there = pl.ds(first + start, rows)
            readout = readout_ref[there, :]
            across = mm(jnp.concatenate([readout, readout], axis=1), terms)
            gated = inside_ref[where, :].astype(F32) + share_ref[where, :].astype(F32) * across
            squares = gated.astype(BF16) * gated.astype(BF16)
            mean = jnp.concatenate(
                [mm(squares[:, g : g + group], average) for g in range(0, width, group)], axis=1
            )
            result_ref[there, :] = (gated * lax.rsqrt(mean + EPSILON) * gain).astype(BF16)
            copy = pltpu.make_async_copy(result_ref.at[there], result_hbm.at[there], semaphores.at[len(copies)])
            copy.start()
            copies.append(copy)
        first += inside_ref.shape[0]
    for copy in copies:
        copy.wait()


def final_part(place, incoming, readout, norm_gain, groups, head_size, cuts):
    length, state_size = readout.shape
    width = norm_gain.shape[1]
    arguments = [place, *incoming, readout, norm_gain, *[v for g in groups for v in g]]
    return pl.pallas_call(
        functools.partial(final_kernel, len(incoming), head_size, len(groups), cuts),
        in_specs=[pl.BlockSpec(memory_space=pltpu.SMEM)] + [IN_VMEM] * (len(arguments) - 1),
        out_specs=IN_HBM,
        out_shape=jax.ShapeDtypeStruct((length, width), BF16),
        scratch_shapes=[
            pltpu.VMEM((length, width), BF16),
            pltpu.VMEM((2 * state_size, width), BF16),
            pltpu.SemaphoreType.DMA((len(groups) * cuts,)),
        ],
        name="final_part",
        compiler_params=pltpu.CompilerParams(vmem_limit_bytes=16 << 20),
        cost_estimate=pl.CostEstimate(
            flops=4 * length * width * state_size,
            bytes_accessed=2 * length * (3 * width + state_size),
            transcendentals=length * width,
        ),
    )(*arguments)


def blend_kernel(place_ref, one_ref, two_ref, own_ref, first_ref, second_ref, kept_ref):
    size = kept_ref.shape[0]
    width = kept_ref.shape[1]

    def scaled(rows_ref, value):
        gain = rows_ref[size:, :]
        shape = (size // HEAD_ROWS, HEAD_ROWS, width)
        return (value.reshape(shape) * gain[None]).reshape(size, width)

    @pl.when(place_ref[0] == 1)
    def _():
        mine = own_ref.at[0]
        first = one_ref[:size, :]
        second = mine[:size, :] + scaled(mine, first)
        first_ref[...] = second
        second_ref[...] = two_ref[:size, :] + scaled(two_ref, second)
        kept_ref[...] = first

    @pl.when(place_ref[0] != 1)
    def _():
        mine = own_ref.at[1]
        first = two_ref[:size, :]
        second = one_ref[:size, :] + scaled(one_ref, first)
        second_ref[...] = second
        kept_ref[...] = second

        @pl.when(place_ref[0] == 0)
        def _():
            first_ref[...] = mine[:size, :]

        @pl.when(place_ref[0] != 0)
        def _():
            first_ref[...] = mine[:size, :] + scaled(mine, second)


def blend(place, one, two, own):
    size = one.shape[0] - HEAD_ROWS
    width = one.shape[1]
    return pl.pallas_call(
        blend_kernel,
        in_specs=[pl.BlockSpec(memory_space=pltpu.SMEM)] + [IN_VMEM] * 3,
        out_specs=[IN_VMEM] * 3,
        out_shape=[pltpu.VMEM((size, width), F32)] * 3,
        name="blend",
        compiler_params=pltpu.CompilerParams(vmem_limit_bytes=4 << 20),
    )(place, one, two, own)


def scan_devices(own, devices):
    size = own.shape[0] - HEAD_ROWS
    gain = lambda v: v[size : size + 1]
    reach, before = own, None
    shift = 1
    while shift < devices:
        came = lax.ppermute(reach, "tm", [(i, i + shift) for i in range(devices - shift)])
        join = lambda later: jnp.concatenate(
            [later[:size] + gain(later) * came[:size], later[size:] * came[size:]], axis=0
        )
        before = came if before is None else join(before)
        reach = join(reach)
        shift *= 2
    if before is None:
        return jnp.zeros_like(own[:size])
    return before[:size]


def shards(devices, signal, entry_map, readout, gate_input, log_decay, norm_gain):
    heads, length = log_decay.shape
    width = signal.shape[1]
    head_size = width // heads
    split = devices == 4 and width % 256 == 0
    early = length * 9 // 16
    late = length - early
    decay = log_decay
    if heads < HEAD_ROWS:
        decay = jnp.pad(log_decay, ((0, HEAD_ROWS - heads), (0, 0)))
    place = lax.axis_index("tm").astype(jnp.int32).reshape(1)
    *made, entry_map, signal, gate_first = local_states(
        place, decay, entry_map, signal, gate_input, head_size, split, 4, early
    )
    common = (entry_map, signal)
    nothing = jnp.zeros((8, 128), F32)
    if split:
        own, first, second = made
        one = lax.ppermute(first, "tm", [(0, 1), (1, 2)])
        two = lax.ppermute(second, "tm", [(2, 1), (0, 2)])
    *before, state = local_part(0, early, decay, readout, gate_first, *common, nothing, head_size, early // (2 * CHUNK))
    if split:
        one, two, state = lax.optimization_barrier((one, two, state))
        first, second, kept = blend(place, one, two, own)
        one = lax.ppermute(first, "tm", [(0, 1), (1, 2), (2, 3)])
        two = lax.ppermute(second, "tm", [(1, 3)])
        incoming = (one, two, kept)
    else:
        incoming = (scan_devices(made[0], devices),)
    *after, _ = local_part(early, late, decay, readout, gate_input, *common, state, head_size, 8)
    gain = norm_gain.reshape(1, width)
    return final_part(place, incoming, readout, gain, (before, after), head_size, 4)


def solution(mesh):
    in_specs = (
        P(("parts", "tm"), ("head", "sub")),
        P(("parts", "tm"), None),
        P(("parts", "tm"), None),
        P(("parts", "tm"), ("head", "sub")),
        P(("head", "sub"), ("parts", "tm")),
        P(("head", "sub")),
    )
    out_specs = P(("parts", "tm"), ("head", "sub"))
    body = functools.partial(shards, mesh.shape["tm"])
    return jax.shard_map(body, mesh=mesh, in_specs=in_specs, out_specs=out_specs, check_vma=False)
```

```python
import functools

import jax
import jax.numpy as jnp
from jax import lax
from jax.experimental import pallas as pl
from jax.experimental.pallas import tpu as pltpu
from jax.sharding import PartitionSpec as P

CHUNK = 128
HEAD_ROWS = 8
EPSILON = 1e-05
F32 = jnp.float32
BF16 = jnp.bfloat16
TN = (((0,), (0,)), ((), ()))
NT = (((1,), (1,)), ((), ()))
IN_HBM = pl.BlockSpec(memory_space=pltpu.HBM)
IN_VMEM = pl.BlockSpec(memory_space=pltpu.VMEM)


def mm(left, right, dims=(((1,), (0,)), ((), ()))):
    return lax.dot_general(left, right, dims, preferred_element_type=F32)


def two_terms(value):
    high = value.astype(BF16)
    return high, (value - high.astype(F32)).astype(BF16)


def spread_matrix(width, head_size):
    row = lax.broadcasted_iota(jnp.int32, (2 * HEAD_ROWS, width), 0)
    column = lax.broadcasted_iota(jnp.int32, (2 * HEAD_ROWS, width), 1)
    own = lax.rem(row, HEAD_ROWS) == lax.div(column, head_size)
    return own.astype(F32).astype(BF16)


def stacked(decay):
    chunks = decay.shape[1] // CHUNK
    return jnp.concatenate([decay[:, c * CHUNK : (c + 1) * CHUNK] for c in range(chunks)], axis=0)


def sums(decay_rows, matrix):
    high = decay_rows.astype(BF16)
    rest = decay_rows - high.astype(F32)
    middle = rest.astype(BF16)
    low = (rest - middle.astype(F32)).astype(BF16)
    return mm(high, matrix) + (mm(middle, matrix) + mm(low, matrix))


def pair_rows(value):
    high, low = two_terms(value)
    return jnp.concatenate([high, low], axis=0)


def indicator(test):
    return test.astype(F32).astype(BF16)


def spread_rows(factor_ref, chunks, spread):
    return jnp.concatenate([mm(factor_ref[c], spread, TN) for c in chunks], axis=0)


def copy_rows(source, target, semaphore, start, rows):
    where = pl.ds(start, rows)
    return pltpu.make_async_copy(source.at[where], target.at[where], semaphore)


def state_kernel(split, head_size, pieces, place_ref, decay_hbm, entry_hbm, signal_hbm, gate_hbm, *rest):
    outs, (entry_ref, signal_ref, gate_ref, decay_ref, factor_ref, semaphores) = rest[:-6], rest[-6:]
    length, width = signal_ref.shape
    rows = length // pieces
    chunks = length // CHUNK
    decay_copy = pltpu.make_async_copy(decay_hbm, decay_ref, semaphores.at[2 * pieces])
    decay_copy.start()
    copies = []
    for k in range(pieces):
        copies.append(copy_rows(entry_hbm, entry_ref, semaphores.at[k], k * rows, rows))
        copies.append(copy_rows(signal_hbm, signal_ref, semaphores.at[pieces + k], k * rows, rows))
    for copy in copies:
        copy.start()
    gate_copy = pltpu.make_async_copy(
        gate_hbm.at[pl.ds(0, gate_ref.shape[0])], gate_ref, semaphores.at[2 * pieces + 1]
    )
    gate_copy.start()
    spread = spread_matrix(width, head_size)
    decay_copy.wait()
    tall = stacked(decay_ref[...])
    s_from = lax.broadcasted_iota(jnp.int32, (CHUNK, 2 * CHUNK), 0)
    s_to = lax.broadcasted_iota(jnp.int32, (CHUNK, 2 * CHUNK), 1)
    both = sums(tall, indicator((s_from > s_to) | (s_to >= CHUNK)))
    later = jnp.zeros((HEAD_ROWS, CHUNK), F32)
    for c in reversed(range(chunks)):
        part = both[c * HEAD_ROWS : (c + 1) * HEAD_ROWS]
        factor_ref[c] = pair_rows(jnp.exp(part[:, :CHUNK] + later))
        later = later + part[:, CHUNK:]
    gain = mm(pair_rows(jnp.exp(later[:, :HEAD_ROWS])), spread, TN)
    states = None
    for k in range(pieces):
        copies[2 * k].wait()
        copies[2 * k + 1].wait()
        where = pl.ds(k * rows, rows)
        here = range(k * rows // CHUNK, (k + 1) * rows // CHUNK)
        scaled = (signal_ref[where, :].astype(F32) * spread_rows(factor_ref, here, spread)).astype(BF16)
        term = mm(entry_ref[where, :], scaled, TN)
        states = term if states is None else states + term
    size = states.shape[0]
    if split:
        own_ref, first_ref, second_ref = outs
        half = width // 2
        for k in range(2):
            own_ref[k, :size, :] = states[:, k * half : (k + 1) * half]
            own_ref[k, size:, :] = gain[:, k * half : (k + 1) * half]

        @pl.when(place_ref[0] == 0)
        def _():
            first_ref[...] = own_ref[0]
            second_ref[...] = own_ref[1]

        @pl.when(place_ref[0] != 0)
        def _():
            first_ref[...] = own_ref[1]
            second_ref[...] = own_ref[0]
    else:
        (own_ref,) = outs
        own_ref[:size, :] = states
        own_ref[size:, :] = gain
    gate_copy.wait()


def local_states(place, decay, entry_map, signal, gate_input, head_size, split, pieces, gate_rows):
    length, width = signal.shape
    state_size = entry_map.shape[1]
    tall = state_size + HEAD_ROWS
    if split:
        shapes = [(2, tall, width // 2), (tall, width // 2), (tall, width // 2)]
    else:
        shapes = [(tall, width)]
    return pl.pallas_call(
        functools.partial(state_kernel, split, head_size, pieces),
        in_specs=[pl.BlockSpec(memory_space=pltpu.SMEM)] + [IN_HBM] * 4,
        out_specs=[IN_VMEM] * (len(shapes) + 3),
        out_shape=[pltpu.VMEM(s, F32) for s in shapes]
        + [
            pltpu.VMEM((length, state_size), BF16),
            pltpu.VMEM((length, width), BF16),
            pltpu.VMEM((gate_rows, width), BF16),
        ],
        scratch_shapes=[
            pltpu.VMEM((HEAD_ROWS, length), F32),
            pltpu.VMEM((length // CHUNK, 2 * HEAD_ROWS, CHUNK), BF16),
            pltpu.SemaphoreType.DMA((2 * pieces + 2,)),
        ],
        name="device_states",
        compiler_params=pltpu.CompilerParams(vmem_limit_bytes=52 << 20),
        cost_estimate=pl.CostEstimate(
            flops=2 * length * width * state_size,
            bytes_accessed=2 * length * (width + state_size),
            transcendentals=0,
        ),
    )(place, decay, entry_map, signal, gate_input)


def by_head(value, factor):
    rows, width = value.shape
    return (value.reshape(rows // HEAD_ROWS, HEAD_ROWS, width) * factor[None]).reshape(rows, width)


def local_kernel(base, head_size, group, decay_ref, readout_ref, gate_ref, entry_ref, signal_ref, state_in, *rest):
    inside_ref, share_ref, state_ref, in_ref, out_ref = rest
    length, width = signal_ref.shape
    part_rows = inside_ref.shape[0]
    first = base // CHUNK
    many = part_rows // CHUNK
    spread = spread_matrix(width, head_size)
    needed = min(first + many + 1, length // CHUNK)
    tall = stacked(decay_ref[:, : needed * CHUNK])
    half = CHUNK // 2
    s_from = lax.broadcasted_iota(jnp.int32, (CHUNK, CHUNK), 0)
    s_to = lax.broadcasted_iota(jnp.int32, (CHUNK, CHUNK), 1)
    early = (s_from < half).astype(F32)
    centred = ((s_from <= s_to).astype(F32) - early).astype(BF16)
    halves = sums(tall, jnp.concatenate([early.astype(BF16), (1.0 - early).astype(BF16)], axis=1))
    inner = sums(tall[first * HEAD_ROWS : (first + many) * HEAD_ROWS], centred)
    before = jnp.zeros((HEAD_ROWS, HEAD_ROWS), F32)
    to_here, to_next = [], []
    for c in range(first + many):
        part = halves[c * HEAD_ROWS : (c + 1) * HEAD_ROWS]
        to_middle = part[:, :HEAD_ROWS]
        onward = part[:, CHUNK : CHUNK + HEAD_ROWS]
        if c >= first:
            from_middle = inner[(c - first) * HEAD_ROWS : (c - first + 1) * HEAD_ROWS]
            frames = slice((c - first) * CHUNK, (c - first + 1) * CHUNK)
            in_ref[:, frames] = pair_rows(jnp.exp(-from_middle))
            out_ref[:, frames] = pair_rows(jnp.exp(from_middle))
            to_here.append(pair_rows(jnp.exp(before + to_middle)))
            if (c + 1) * CHUNK < length:
                following = halves[(c + 1) * HEAD_ROWS : (c + 2) * HEAD_ROWS, :HEAD_ROWS]
                to_next.append(pair_rows(jnp.exp(onward + following)))
            else:
                to_next.append(pair_rows(jnp.exp(onward)))
        before = before + (to_middle + onward)
    causal = s_from >= s_to
    state = state_in[...] if base else jnp.zeros(state_ref.shape, F32)
    for start in range(0, many, group):
        count = min(group, many - start)
        where = pl.ds(base + start * CHUNK, count * CHUNK)
        there = pl.ds(start * CHUNK, count * CHUNK)
        cut = lambda value, j: value[j * CHUNK : (j + 1) * CHUNK]
        entry = entry_ref[where, :]
        readout = readout_ref[where, :]
        scaled = (signal_ref[where, :].astype(F32) * mm(in_ref[:, there], spread, TN)).astype(BF16)
        scores, added, passed = [], [], []
        for j in range(count):
            products = mm(cut(readout, j), cut(entry, j), NT)
            scores.append(jnp.where(causal, products, 0.0).astype(BF16))
            added.append(mm(cut(entry, j), cut(scaled, j), TN))
        for j in range(count):
            passed.append(state.astype(BF16))
            state = by_head(state + added[j], mm(to_next[start + j], spread, TN))
        output = jnp.concatenate(
            [
                mm(
                    jnp.concatenate([scores[j], cut(readout, j)], axis=1),
                    jnp.concatenate([cut(scaled, j), passed[j]], axis=0),
                )
                for j in range(count)
            ],
            axis=0,
        )
        gate = gate_ref[there if gate_ref.shape[0] == part_rows else where, :].astype(F32)
        opened = gate / (1.0 + jnp.exp(-gate)) * mm(out_ref[:, there], spread, TN)
        inside_ref[there, :] = (output * opened).astype(BF16)
        share_ref[there, :] = jnp.concatenate(
            [by_head(cut(opened, j), mm(to_here[start + j], spread, TN)) for j in range(count)], axis=0
        ).astype(BF16)
    state_ref[...] = state


def local_part(base, rows, decay, readout, gate_input, entry_map, signal, state, head_size, group):
    length, width = signal.shape
    state_size = entry_map.shape[1]
    return pl.pallas_call(
        functools.partial(local_kernel, base, head_size, group),
        in_specs=[IN_VMEM] * 6,
        out_specs=[IN_VMEM] * 3,
        out_shape=[pltpu.VMEM((rows, width), BF16)] * 2 + [pltpu.VMEM((state_size, width), F32)],
        scratch_shapes=[pltpu.VMEM((2 * HEAD_ROWS, rows), BF16)] * 2,
        name="local_part",
        compiler_params=pltpu.CompilerParams(vmem_limit_bytes=16 << 20),
        cost_estimate=pl.CostEstimate(
            flops=8 * rows * width * state_size,
            bytes_accessed=2 * rows * (4 * width + 2 * state_size),
            transcendentals=rows * width,
        ),
    )(decay, readout, gate_input, entry_map, signal, state)


def final_kernel(count, head_size, parts, cuts, place_ref, *rest):
    incoming, rest = rest[:count], rest[count:]
    readout_ref, gain_ref, *rest = rest
    groups, rest = [rest[2 * p : 2 * p + 2] for p in range(parts)], rest[2 * parts :]
    result_hbm, result_ref, terms_ref, semaphores = rest
    size = readout_ref.shape[1]
    width = gain_ref.shape[1]

    def keep(value_ref, at):
        high, low = two_terms(value_ref[...])
        terms_ref[:size, at : at + value_ref.shape[1]] = high
        terms_ref[size:, at : at + value_ref.shape[1]] = low

    if count == 1:
        keep(incoming[0], 0)
    else:
        one, two, kept = incoming
        place = place_ref[0]
        half = width // 2

        @pl.when(place == 1)
        def _():
            keep(kept, 0)
            keep(one, half)

        @pl.when(place == 2)
        def _():
            keep(one, 0)
            keep(kept, half)

        @pl.when((place != 1) & (place != 2))
        def _():
            keep(two, 0)
            keep(one, half)

    group = min(width, 256)
    row = lax.broadcasted_iota(jnp.int32, (group, group), 0)
    column = lax.broadcasted_iota(jnp.int32, (group, group), 1)
    same = lax.div(row, head_size) == lax.div(column, head_size)
    average = jnp.where(same, 1.0 / head_size, 0.0).astype(BF16)
    gain = gain_ref[...]
    terms = terms_ref[...]
    copies = []
    first = 0
    for inside_ref, share_ref in groups:
        rows = inside_ref.shape[0] // cuts
        for start in range(0, inside_ref.shape[0], rows):
            where = pl.ds(start, rows)
            there = pl.ds(first + start, rows)
            readout = readout_ref[there, :]
            across = mm(jnp.concatenate([readout, readout], axis=1), terms)
            gated = inside_ref[where, :].astype(F32) + share_ref[where, :].astype(F32) * across
            squares = gated.astype(BF16) * gated.astype(BF16)
            mean = jnp.concatenate(
                [mm(squares[:, g : g + group], average) for g in range(0, width, group)], axis=1
            )
            result_ref[there, :] = (gated * lax.rsqrt(mean + EPSILON) * gain).astype(BF16)
            copy = pltpu.make_async_copy(result_ref.at[there], result_hbm.at[there], semaphores.at[len(copies)])
            copy.start()
            copies.append(copy)
        first += inside_ref.shape[0]
    for copy in copies:
        copy.wait()


def final_part(place, incoming, readout, norm_gain, groups, head_size, cuts):
    length, state_size = readout.shape
    width = norm_gain.shape[1]
    arguments = [place, *incoming, readout, norm_gain, *[v for g in groups for v in g]]
    return pl.pallas_call(
        functools.partial(final_kernel, len(incoming), head_size, len(groups), cuts),
        in_specs=[pl.BlockSpec(memory_space=pltpu.SMEM)] + [IN_VMEM] * (len(arguments) - 1),
        out_specs=IN_HBM,
        out_shape=jax.ShapeDtypeStruct((length, width), BF16),
        scratch_shapes=[
            pltpu.VMEM((length, width), BF16),
            pltpu.VMEM((2 * state_size, width), BF16),
            pltpu.SemaphoreType.DMA((len(groups) * cuts,)),
        ],
        name="final_part",
        compiler_params=pltpu.CompilerParams(vmem_limit_bytes=16 << 20),
        cost_estimate=pl.CostEstimate(
            flops=4 * length * width * state_size,
            bytes_accessed=2 * length * (3 * width + state_size),
            transcendentals=length * width,
        ),
    )(*arguments)


def blend_kernel(place_ref, one_ref, two_ref, own_ref, first_ref, second_ref, kept_ref):
    size = kept_ref.shape[0]
    width = kept_ref.shape[1]

    def scaled(rows_ref, value):
        gain = rows_ref[size:, :]
        shape = (size // HEAD_ROWS, HEAD_ROWS, width)
        return (value.reshape(shape) * gain[None]).reshape(size, width)

    @pl.when(place_ref[0] == 1)
    def _():
        mine = own_ref.at[0]
        first = one_ref[:size, :]
        second = mine[:size, :] + scaled(mine, first)
        first_ref[...] = second
        second_ref[...] = two_ref[:size, :] + scaled(two_ref, second)
        kept_ref[...] = first

    @pl.when(place_ref[0] != 1)
    def _():
        mine = own_ref.at[1]
        first = two_ref[:size, :]
        second = one_ref[:size, :] + scaled(one_ref, first)
        second_ref[...] = second
        kept_ref[...] = second

        @pl.when(place_ref[0] == 0)
        def _():
            first_ref[...] = mine[:size, :]

        @pl.when(place_ref[0] != 0)
        def _():
            first_ref[...] = mine[:size, :] + scaled(mine, second)


def blend(place, one, two, own):
    size = one.shape[0] - HEAD_ROWS
    width = one.shape[1]
    return pl.pallas_call(
        blend_kernel,
        in_specs=[pl.BlockSpec(memory_space=pltpu.SMEM)] + [IN_VMEM] * 3,
        out_specs=[IN_VMEM] * 3,
        out_shape=[pltpu.VMEM((size, width), F32)] * 3,
        name="blend",
        compiler_params=pltpu.CompilerParams(vmem_limit_bytes=4 << 20),
    )(place, one, two, own)


def scan_devices(own, devices):
    size = own.shape[0] - HEAD_ROWS
    gain = lambda v: v[size : size + 1]
    reach, before = own, None
    shift = 1
    while shift < devices:
        came = lax.ppermute(reach, "tm", [(i, i + shift) for i in range(devices - shift)])
        join = lambda later: jnp.concatenate(
            [later[:size] + gain(later) * came[:size], later[size:] * came[size:]], axis=0
        )
        before = came if before is None else join(before)
        reach = join(reach)
        shift *= 2
    if before is None:
        return jnp.zeros_like(own[:size])
    return before[:size]


def shards(devices, signal, entry_map, readout, gate_input, log_decay, norm_gain):
    heads, length = log_decay.shape
    width = signal.shape[1]
    head_size = width // heads
    split = devices == 4 and width % 256 == 0
    early = length * 9 // 16
    late = length - early
    decay = log_decay
    if heads < HEAD_ROWS:
        decay = jnp.pad(log_decay, ((0, HEAD_ROWS - heads), (0, 0)))
    place = lax.axis_index("tm").astype(jnp.int32).reshape(1)
    *made, entry_map, signal, gate_first = local_states(
        place, decay, entry_map, signal, gate_input, head_size, split, 4, early
    )
    common = (entry_map, signal)
    nothing = jnp.zeros((8, 128), F32)
    if split:
        own, first, second = made
        one = lax.ppermute(first, "tm", [(0, 1), (1, 2)])
        two = lax.ppermute(second, "tm", [(2, 1), (0, 2)])
    *before, state = local_part(0, early, decay, readout, gate_first, *common, nothing, head_size, early // (2 * CHUNK))
    if split:
        one, two, state = lax.optimization_barrier((one, two, state))
        first, second, kept = blend(place, one, two, own)
        one = lax.ppermute(first, "tm", [(0, 1), (1, 2), (2, 3)])
        two = lax.ppermute(second, "tm", [(1, 3)])
        incoming = (one, two, kept)
    else:
        incoming = (scan_devices(made[0], devices),)
    *after, _ = local_part(early, late, decay, readout, gate_input, *common, state, head_size, 8)
    gain = norm_gain.reshape(1, width)
    return final_part(place, incoming, readout, gain, (before, after), head_size, 4)


def solution(mesh):
    in_specs = (
        P(("parts", "tm"), ("head", "sub")),
        P(("parts", "tm"), None),
        P(("parts", "tm"), None),
        P(("parts", "tm"), ("head", "sub")),
        P(("head", "sub"), ("parts", "tm")),
        P(("head", "sub")),
    )
    out_specs = P(("parts", "tm"), ("head", "sub"))
    body = functools.partial(shards, mesh.shape["tm"])
    return jax.shard_map(body, mesh=mesh, in_specs=in_specs, out_specs=out_specs, check_vma=False)
```

```python
import functools

import jax
import jax.numpy as jnp
from jax import lax
from jax.experimental import pallas as pl
from jax.experimental.pallas import tpu as pltpu
from jax.sharding import PartitionSpec as P

CHUNK = 128
HEAD_ROWS = 8
EPSILON = 1e-05
F32 = jnp.float32
BF16 = jnp.bfloat16
TN = (((0,), (0,)), ((), ()))
NT = (((1,), (1,)), ((), ()))
IN_HBM = pl.BlockSpec(memory_space=pltpu.HBM)
IN_VMEM = pl.BlockSpec(memory_space=pltpu.VMEM)


def mm(left, right, dims=(((1,), (0,)), ((), ()))):
    return lax.dot_general(left, right, dims, preferred_element_type=F32)


def two_terms(value):
    high = value.astype(BF16)
    return high, (value - high.astype(F32)).astype(BF16)


def spread_matrix(width, head_size):
    row = lax.broadcasted_iota(jnp.int32, (2 * HEAD_ROWS, width), 0)
    column = lax.broadcasted_iota(jnp.int32, (2 * HEAD_ROWS, width), 1)
    own = lax.rem(row, HEAD_ROWS) == lax.div(column, head_size)
    return own.astype(F32).astype(BF16)


def stacked(decay):
    chunks = decay.shape[1] // CHUNK
    return jnp.concatenate([decay[:, c * CHUNK : (c + 1) * CHUNK] for c in range(chunks)], axis=0)


def sums(decay_rows, matrix):
    high = decay_rows.astype(BF16)
    rest = decay_rows - high.astype(F32)
    middle = rest.astype(BF16)
    low = (rest - middle.astype(F32)).astype(BF16)
    return mm(high, matrix) + (mm(middle, matrix) + mm(low, matrix))


def pair_rows(value):
    high, low = two_terms(value)
    return jnp.concatenate([high, low], axis=0)


def indicator(test):
    return test.astype(F32).astype(BF16)


def spread_rows(factor_ref, chunks, spread):
    return jnp.concatenate([mm(factor_ref[c], spread, TN) for c in chunks], axis=0)


def copy_rows(source, target, semaphore, start, rows):
    where = pl.ds(start, rows)
    return pltpu.make_async_copy(source.at[where], target.at[where], semaphore)


def state_kernel(split, head_size, pieces, place_ref, decay_hbm, entry_hbm, signal_hbm, gate_hbm, *rest):
    outs, (entry_ref, signal_ref, gate_ref, decay_ref, factor_ref, semaphores) = rest[:-6], rest[-6:]
    length, width = signal_ref.shape
    rows = length // pieces
    chunks = length // CHUNK
    decay_copy = pltpu.make_async_copy(decay_hbm, decay_ref, semaphores.at[2 * pieces])
    decay_copy.start()
    copies = []
    for k in range(pieces):
        copies.append(copy_rows(entry_hbm, entry_ref, semaphores.at[k], k * rows, rows))
        copies.append(copy_rows(signal_hbm, signal_ref, semaphores.at[pieces + k], k * rows, rows))
    for copy in copies:
        copy.start()
    gate_copy = pltpu.make_async_copy(
        gate_hbm.at[pl.ds(0, gate_ref.shape[0])], gate_ref, semaphores.at[2 * pieces + 1]
    )
    gate_copy.start()
    spread = spread_matrix(width, head_size)
    decay_copy.wait()
    tall = stacked(decay_ref[...])
    s_from = lax.broadcasted_iota(jnp.int32, (CHUNK, 2 * CHUNK), 0)
    s_to = lax.broadcasted_iota(jnp.int32, (CHUNK, 2 * CHUNK), 1)
    both = sums(tall, indicator((s_from > s_to) | (s_to >= CHUNK)))
    later = jnp.zeros((HEAD_ROWS, CHUNK), F32)
    for c in reversed(range(chunks)):
        part = both[c * HEAD_ROWS : (c + 1) * HEAD_ROWS]
        factor_ref[c] = pair_rows(jnp.exp(part[:, :CHUNK] + later))
        later = later + part[:, CHUNK:]
    gain = mm(pair_rows(jnp.exp(later[:, :HEAD_ROWS])), spread, TN)
    states = None
    for k in range(pieces):
        copies[2 * k].wait()
        copies[2 * k + 1].wait()
        where = pl.ds(k * rows, rows)
        here = range(k * rows // CHUNK, (k + 1) * rows // CHUNK)
        scaled = (signal_ref[where, :].astype(F32) * spread_rows(factor_ref, here, spread)).astype(BF16)
        term = mm(entry_ref[where, :], scaled, TN)
        states = term if states is None else states + term
    size = states.shape[0]
    if split:
        own_ref, first_ref, second_ref = outs
        half = width // 2
        for k in range(2):
            own_ref[k, :size, :] = states[:, k * half : (k + 1) * half]
            own_ref[k, size:, :] = gain[:, k * half : (k + 1) * half]

        def fill(ref, k):
            ref[:size, :] = states[:, k * half : (k + 1) * half]
            ref[size:, :] = gain[:, k * half : (k + 1) * half]

        @pl.when(place_ref[0] == 0)
        def _():
            fill(first_ref, 0)
            fill(second_ref, 1)

        @pl.when(place_ref[0] != 0)
        def _():
            fill(first_ref, 1)
            fill(second_ref, 0)
    else:
        (own_ref,) = outs
        own_ref[:size, :] = states
        own_ref[size:, :] = gain
    gate_copy.wait()


def local_states(place, decay, entry_map, signal, gate_input, head_size, split, pieces, gate_rows):
    length, width = signal.shape
    state_size = entry_map.shape[1]
    tall = state_size + HEAD_ROWS
    if split:
        shapes = [(2, tall, width // 2), (tall, width // 2), (tall, width // 2)]
    else:
        shapes = [(tall, width)]
    return pl.pallas_call(
        functools.partial(state_kernel, split, head_size, pieces),
        in_specs=[pl.BlockSpec(memory_space=pltpu.SMEM)] + [IN_HBM] * 4,
        out_specs=[IN_VMEM] * (len(shapes) + 3),
        out_shape=[pltpu.VMEM(s, F32) for s in shapes]
        + [
            pltpu.VMEM((length, state_size), BF16),
            pltpu.VMEM((length, width), BF16),
            pltpu.VMEM((gate_rows, width), BF16),
        ],
        scratch_shapes=[
            pltpu.VMEM((HEAD_ROWS, length), F32),
            pltpu.VMEM((length // CHUNK, 2 * HEAD_ROWS, CHUNK), BF16),
            pltpu.SemaphoreType.DMA((2 * pieces + 2,)),
        ],
        name="device_states",
        compiler_params=pltpu.CompilerParams(vmem_limit_bytes=52 << 20),
        cost_estimate=pl.CostEstimate(
            flops=2 * length * width * state_size,
            bytes_accessed=2 * length * (width + state_size),
            transcendentals=0,
        ),
    )(place, decay, entry_map, signal, gate_input)


def by_head(value, factor):
    rows, width = value.shape
    return (value.reshape(rows // HEAD_ROWS, HEAD_ROWS, width) * factor[None]).reshape(rows, width)


def local_kernel(base, head_size, group, decay_ref, readout_ref, gate_ref, entry_ref, signal_ref, state_in, *rest):
    inside_ref, share_ref, state_ref, in_ref, out_ref = rest
    length, width = signal_ref.shape
    part_rows = inside_ref.shape[0]
    first = base // CHUNK
    many = part_rows // CHUNK
    spread = spread_matrix(width, head_size)
    needed = min(first + many + 1, length // CHUNK)
    tall = stacked(decay_ref[:, : needed * CHUNK])
    half = CHUNK // 2
    s_from = lax.broadcasted_iota(jnp.int32, (CHUNK, CHUNK), 0)
    s_to = lax.broadcasted_iota(jnp.int32, (CHUNK, CHUNK), 1)
    early = (s_from < half).astype(F32)
    centred = ((s_from <= s_to).astype(F32) - early).astype(BF16)
    halves = sums(tall, jnp.concatenate([early.astype(BF16), (1.0 - early).astype(BF16)], axis=1))
    inner = sums(tall[first * HEAD_ROWS : (first + many) * HEAD_ROWS], centred)
    before = jnp.zeros((HEAD_ROWS, HEAD_ROWS), F32)
    to_here, to_next = [], []
    for c in range(first + many):
        part = halves[c * HEAD_ROWS : (c + 1) * HEAD_ROWS]
        to_middle = part[:, :HEAD_ROWS]
        onward = part[:, CHUNK : CHUNK + HEAD_ROWS]
        if c >= first:
            from_middle = inner[(c - first) * HEAD_ROWS : (c - first + 1) * HEAD_ROWS]
            frames = slice((c - first) * CHUNK, (c - first + 1) * CHUNK)
            in_ref[:, frames] = pair_rows(jnp.exp(-from_middle))
            out_ref[:, frames] = pair_rows(jnp.exp(from_middle))
            to_here.append(pair_rows(jnp.exp(before + to_middle)))
            if (c + 1) * CHUNK < length:
                following = halves[(c + 1) * HEAD_ROWS : (c + 2) * HEAD_ROWS, :HEAD_ROWS]
                to_next.append(pair_rows(jnp.exp(onward + following)))
            else:
                to_next.append(pair_rows(jnp.exp(onward)))
        before = before + (to_middle + onward)
    causal = s_from >= s_to
    state = state_in[...] if base else jnp.zeros(state_ref.shape, F32)
    for start in range(0, many, group):
        count = min(group, many - start)
        where = pl.ds(base + start * CHUNK, count * CHUNK)
        there = pl.ds(start * CHUNK, count * CHUNK)
        cut = lambda value, j: value[j * CHUNK : (j + 1) * CHUNK]
        entry = entry_ref[where, :]
        readout = readout_ref[where, :]
        scaled = (signal_ref[where, :].astype(F32) * mm(in_ref[:, there], spread, TN)).astype(BF16)
        scores, added, passed = [], [], []
        for j in range(count):
            products = mm(cut(readout, j), cut(entry, j), NT)
            scores.append(jnp.where(causal, products, 0.0).astype(BF16))
            added.append(mm(cut(entry, j), cut(scaled, j), TN))
        for j in range(count):
            passed.append(state.astype(BF16))
            state = by_head(state + added[j], mm(to_next[start + j], spread, TN))
        output = jnp.concatenate(
            [
                mm(
                    jnp.concatenate([scores[j], cut(readout, j)], axis=1),
                    jnp.concatenate([cut(scaled, j), passed[j]], axis=0),
                )
                for j in range(count)
            ],
            axis=0,
        )
        gate = gate_ref[there if gate_ref.shape[0] == part_rows else where, :].astype(F32)
        opened = gate / (1.0 + jnp.exp(-gate)) * mm(out_ref[:, there], spread, TN)
        inside_ref[there, :] = (output * opened).astype(BF16)
        share_ref[there, :] = jnp.concatenate(
            [by_head(cut(opened, j), mm(to_here[start + j], spread, TN)) for j in range(count)], axis=0
        ).astype(BF16)
    state_ref[...] = state


def local_part(base, rows, decay, readout, gate_input, entry_map, signal, state, head_size, group):
    length, width = signal.shape
    state_size = entry_map.shape[1]
    return pl.pallas_call(
        functools.partial(local_kernel, base, head_size, group),
        in_specs=[IN_VMEM] * 6,
        out_specs=[IN_VMEM] * 3,
        out_shape=[pltpu.VMEM((rows, width), BF16)] * 2 + [pltpu.VMEM((state_size, width), F32)],
        scratch_shapes=[pltpu.VMEM((2 * HEAD_ROWS, rows), BF16)] * 2,
        name="local_part",
        compiler_params=pltpu.CompilerParams(vmem_limit_bytes=16 << 20),
        cost_estimate=pl.CostEstimate(
            flops=8 * rows * width * state_size,
            bytes_accessed=2 * rows * (4 * width + 2 * state_size),
            transcendentals=rows * width,
        ),
    )(decay, readout, gate_input, entry_map, signal, state)


def final_kernel(count, head_size, parts, cuts, place_ref, *rest):
    incoming, rest = rest[:count], rest[count:]
    readout_ref, gain_ref, *rest = rest
    groups, rest = [rest[2 * p : 2 * p + 2] for p in range(parts)], rest[2 * parts :]
    result_hbm, result_ref, terms_ref, semaphores = rest
    size = readout_ref.shape[1]
    width = gain_ref.shape[1]

    def keep(value_ref, at):
        high, low = two_terms(value_ref[...])
        terms_ref[:size, at : at + value_ref.shape[1]] = high
        terms_ref[size:, at : at + value_ref.shape[1]] = low

    if count == 1:
        keep(incoming[0], 0)
    else:
        one, two, kept = incoming
        place = place_ref[0]
        half = width // 2

        @pl.when(place == 1)
        def _():
            keep(kept, 0)
            keep(one, half)

        @pl.when(place == 2)
        def _():
            keep(one, 0)
            keep(kept, half)

        @pl.when((place != 1) & (place != 2))
        def _():
            keep(two, 0)
            keep(one, half)

    group = min(width, 256)
    row = lax.broadcasted_iota(jnp.int32, (group, group), 0)
    column = lax.broadcasted_iota(jnp.int32, (group, group), 1)
    same = lax.div(row, head_size) == lax.div(column, head_size)
    average = jnp.where(same, 1.0 / head_size, 0.0).astype(BF16)
    gain = gain_ref[...]
    terms = terms_ref[...]
    copies = []
    first = 0
    for inside_ref, share_ref in groups:
        rows = inside_ref.shape[0] // cuts
        for start in range(0, inside_ref.shape[0], rows):
            where = pl.ds(start, rows)
            there = pl.ds(first + start, rows)
            readout = readout_ref[there, :]
            across = mm(jnp.concatenate([readout, readout], axis=1), terms)
            gated = inside_ref[where, :].astype(F32) + share_ref[where, :].astype(F32) * across
            squares = gated.astype(BF16) * gated.astype(BF16)
            mean = jnp.concatenate(
                [mm(squares[:, g : g + group], average) for g in range(0, width, group)], axis=1
            )
            result_ref[there, :] = (gated * lax.rsqrt(mean + EPSILON) * gain).astype(BF16)
            copy = pltpu.make_async_copy(result_ref.at[there], result_hbm.at[there], semaphores.at[len(copies)])
            copy.start()
            copies.append(copy)
        first += inside_ref.shape[0]
    for copy in copies:
        copy.wait()


def final_part(place, incoming, readout, norm_gain, groups, head_size, cuts):
    length, state_size = readout.shape
    width = norm_gain.shape[1]
    arguments = [place, *incoming, readout, norm_gain, *[v for g in groups for v in g]]
    return pl.pallas_call(
        functools.partial(final_kernel, len(incoming), head_size, len(groups), cuts),
        in_specs=[pl.BlockSpec(memory_space=pltpu.SMEM)] + [IN_VMEM] * (len(arguments) - 1),
        out_specs=IN_HBM,
        out_shape=jax.ShapeDtypeStruct((length, width), BF16),
        scratch_shapes=[
            pltpu.VMEM((length, width), BF16),
            pltpu.VMEM((2 * state_size, width), BF16),
            pltpu.SemaphoreType.DMA((len(groups) * cuts,)),
        ],
        name="final_part",
        compiler_params=pltpu.CompilerParams(vmem_limit_bytes=16 << 20),
        cost_estimate=pl.CostEstimate(
            flops=4 * length * width * state_size,
            bytes_accessed=2 * length * (3 * width + state_size),
            transcendentals=length * width,
        ),
    )(*arguments)


def blend_kernel(place_ref, one_ref, two_ref, own_ref, first_ref, second_ref, kept_ref):
    size = kept_ref.shape[0]
    width = kept_ref.shape[1]

    def scaled(rows_ref, value):
        gain = rows_ref[size:, :]
        shape = (size // HEAD_ROWS, HEAD_ROWS, width)
        return (value.reshape(shape) * gain[None]).reshape(size, width)

    @pl.when(place_ref[0] == 1)
    def _():
        mine = own_ref.at[0]
        first = one_ref[:size, :]
        second = mine[:size, :] + scaled(mine, first)
        first_ref[...] = second
        second_ref[...] = two_ref[:size, :] + scaled(two_ref, second)
        kept_ref[...] = first

    @pl.when(place_ref[0] != 1)
    def _():
        mine = own_ref.at[1]
        first = two_ref[:size, :]
        second = one_ref[:size, :] + scaled(one_ref, first)
        second_ref[...] = second
        kept_ref[...] = second

        @pl.when(place_ref[0] == 0)
        def _():
            first_ref[...] = mine[:size, :]

        @pl.when(place_ref[0] != 0)
        def _():
            first_ref[...] = mine[:size, :] + scaled(mine, second)


def blend(place, one, two, own):
    size = one.shape[0] - HEAD_ROWS
    width = one.shape[1]
    return pl.pallas_call(
        blend_kernel,
        in_specs=[pl.BlockSpec(memory_space=pltpu.SMEM)] + [IN_VMEM] * 3,
        out_specs=[IN_VMEM] * 3,
        out_shape=[pltpu.VMEM((size, width), F32)] * 3,
        name="blend",
        compiler_params=pltpu.CompilerParams(vmem_limit_bytes=4 << 20),
    )(place, one, two, own)


def scan_devices(own, devices):
    size = own.shape[0] - HEAD_ROWS
    gain = lambda v: v[size : size + 1]
    reach, before = own, None
    shift = 1
    while shift < devices:
        came = lax.ppermute(reach, "tm", [(i, i + shift) for i in range(devices - shift)])
        join = lambda later: jnp.concatenate(
            [later[:size] + gain(later) * came[:size], later[size:] * came[size:]], axis=0
        )
        before = came if before is None else join(before)
        reach = join(reach)
        shift *= 2
    if before is None:
        return jnp.zeros_like(own[:size])
    return before[:size]


def shards(devices, signal, entry_map, readout, gate_input, log_decay, norm_gain):
    heads, length = log_decay.shape
    width = signal.shape[1]
    head_size = width // heads
    split = devices == 4 and width % 256 == 0
    early = length * 9 // 16
    late = length - early
    decay = log_decay
    if heads < HEAD_ROWS:
        decay = jnp.pad(log_decay, ((0, HEAD_ROWS - heads), (0, 0)))
    place = lax.axis_index("tm").astype(jnp.int32).reshape(1)
    *made, entry_map, signal, gate_first = local_states(
        place, decay, entry_map, signal, gate_input, head_size, split, 4, early
    )
    common = (entry_map, signal)
    nothing = jnp.zeros((8, 128), F32)
    if split:
        own, first, second = made
        one = lax.ppermute(first, "tm", [(0, 1), (1, 2)])
        two = lax.ppermute(second, "tm", [(2, 1), (0, 2)])
    *before, state = local_part(0, early, decay, readout, gate_first, *common, nothing, head_size, early // (2 * CHUNK))
    if split:
        one, two, state = lax.optimization_barrier((one, two, state))
        first, second, kept = blend(place, one, two, own)
        one = lax.ppermute(first, "tm", [(0, 1), (1, 2), (2, 3)])
        two = lax.ppermute(second, "tm", [(1, 3)])
        incoming = (one, two, kept)
    else:
        incoming = (scan_devices(made[0], devices),)
    *after, _ = local_part(early, late, decay, readout, gate_input, *common, state, head_size, 8)
    gain = norm_gain.reshape(1, width)
    return final_part(place, incoming, readout, gain, (before, after), head_size, 4)


def solution(mesh):
    in_specs = (
        P(("parts", "tm"), ("head", "sub")),
        P(("parts", "tm"), None),
        P(("parts", "tm"), None),
        P(("parts", "tm"), ("head", "sub")),
        P(("head", "sub"), ("parts", "tm")),
        P(("head", "sub")),
    )
    out_specs = P(("parts", "tm"), ("head", "sub"))
    body = functools.partial(shards, mesh.shape["tm"])
    return jax.shard_map(body, mesh=mesh, in_specs=in_specs, out_specs=out_specs, check_vma=False)
```
